32 devices in a mesh: sec: 8 (over y, x, core), cross: 4 (over z).
Axes of the slice: x: 2, y: 2, z: 4, core: 2. Of those that a mesh axis runs over, the one named last changes fastest.
Arguments:
- rhs_field: float32 [2, 8, 2, 512, 512], P(None, 'sec', None, 'cross'), may hold values from -1.5 to 1.5
- slowness: float32 [8, 512, 512], P('sec', 'cross'), may hold values from 0.25 to 4
- absorb_depth: int32 [8], P('sec'), may hold values from 8 to 64
- line_inverse: bfloat16 [8, 2, 512, 512], P('sec'), may hold values from -1 to 1
- cross_inverse: bfloat16 [8, 2, 512, 512], P('sec', None, 'cross'), may hold values from -1 to 1
Outputs:
- solution: float32 [2, 8, 2, 512, 512], P(None, 'sec', None, 'cross')
- residual: float32 [2, 8, 2, 512, 512], P(None, 'sec', None, 'cross')
The draws below stay inside these ranges and needn't reach their ends.
All inputs are finite; a program needn't handle non-finite values.
Results may differ from the reference program's by a relative error of at most 0.02.
Values may be sent and summed in bfloat16 or wider, within the bound.
A program may use at most 64 MiB of HBM per device.

```python
import math
import jax
import jax.numpy as jnp
from jax import lax

NX = 512
NY = 512
RHS = 2
LAY = 1
NZ = 8


def assemble(phase_key, magnitude, remainder):
    order = magnitude.shape[-1]
    phase = jax.random.uniform(phase_key, magnitude.shape, jnp.float32, -math.pi, math.pi)
    diagonal = jnp.stack([magnitude * jnp.cos(phase), magnitude * jnp.sin(phase)], axis=1)
    identity = jnp.eye(order, dtype=jnp.float32)
    return remainder * (1.0 - identity) + diagonal[..., None] * identity


def draw_line_inverse(key, part):
    phase_key = jax.random.fold_in(jax.random.fold_in(key, 11), 0)
    remainder_key = jax.random.fold_in(jax.random.fold_in(key, 11), 2)
    sections = NZ // LAY
    magnitude = jnp.full((sections, NX), math.sqrt(0.92), jnp.float32)
    remainder = jax.random.normal(remainder_key, (sections, 2, NX, NX), jnp.float32) * (0.2 / math.sqrt(NX))
    return assemble(phase_key, magnitude, remainder).astype(jnp.bfloat16)


def draw_cross_inverse(key, part):
    phase_key = jax.random.fold_in(jax.random.fold_in(key, 23), 0)
    remainder_key = jax.random.fold_in(jax.random.fold_in(key, 23), 2)
    magnitude = jnp.full((NZ, NY), math.sqrt(0.92), jnp.float32)
    remainder = jax.random.normal(remainder_key, (NZ, 2, NY, NY), jnp.float32) * (0.2 / math.sqrt(NY))
    return assemble(phase_key, magnitude, remainder).astype(jnp.bfloat16)


def draw_absorb_depth(key, part):
    value_key, place_key = jax.random.split(jax.random.fold_in(key, 37))
    depth = jax.random.randint(value_key, (NZ,), 8, 65, dtype=jnp.int32)
    place = jax.random.randint(place_key, (), 0, NZ, dtype=jnp.int32)
    position = jnp.arange(NZ, dtype=jnp.int32)
    depth = jnp.where(position == place, 64, depth)
    depth = jnp.where(position == (place + 1) % NZ, 8, depth)
    return depth


def block_levels(stream_key, extent, cuts, low, largest):
    loudness, own = 1.0, jax.random.fold_in(stream_key, 6)
    for axis_at, shards_of in cuts:
        heights = jnp.exp(jax.random.uniform(jax.random.fold_in(own, axis_at), (shards_of,), jnp.float32, low / len(cuts), largest / len(cuts)))
        loudness = loudness * jnp.repeat(heights, extent[axis_at] // shards_of).reshape([-1 if axis == axis_at else 1 for axis in range(len(extent))])
    return loudness


def centred(stream_key, dims, width, most, pieces=(), kind=jnp.bfloat16):
    entries = jax.random.normal(stream_key, dims, jnp.float32) * width
    if len(pieces) > 0:
        entries = block_levels(stream_key, dims, pieces, -0.22, 0.18) * entries
    return jnp.clip(entries, min=-most, max=most).astype(kind)


def setup_inputs(seed: int = 0) -> dict:
    key_list = jax.random.split(jax.random.key(seed), 6)
    rhs_field = centred(key_list[0], (2, NZ, RHS, NY, NX), 0.25, 1.5, ((1, 8), (3, 4)), jnp.float32)
    slowness = jnp.clip(jnp.exp(math.log(4.0) - 2.7725887 * jax.random.uniform(key_list[1], (NZ, NY, NX), jnp.float32) ** block_levels(key_list[1], (NZ, NY, NX), ((0, 8), (1, 4)), -0.2, 0.2)), 0.25, 4.0)
    absorb_depth = draw_absorb_depth(jax.random.fold_in(key_list[5], 71), 0)
    line_inverse = draw_line_inverse(jax.random.fold_in(key_list[5], 71), 0)
    cross_inverse = draw_cross_inverse(jax.random.fold_in(key_list[5], 71), 0)
    return {"rhs_field": rhs_field, "slowness": slowness, "absorb_depth": absorb_depth, "line_inverse": line_inverse, "cross_inverse": cross_inverse}


SIGMA_TOP = 2.0
CENTER = 128.0 / 30.0
FACE = 14.0 / 30.0
EDGE = 3.0 / 30.0
CORNER = 1.0 / 30.0


def complex_line(source, matrix):
    real_part = jnp.dot(source[0], matrix[0], preferred_element_type=jnp.float32) - jnp.dot(source[1], matrix[1], preferred_element_type=jnp.float32)
    imag_part = jnp.dot(source[0], matrix[1], preferred_element_type=jnp.float32) + jnp.dot(source[1], matrix[0], preferred_element_type=jnp.float32)
    return jnp.stack([real_part, imag_part]).astype(jnp.bfloat16)


def cross_mix(mixed, cross):
    field = mixed.astype(jnp.float32)
    coupling = cross.astype(jnp.float32)
    real_part = jnp.einsum('yk,rkx->ryx', coupling[0], field[0]) - jnp.einsum('yk,rkx->ryx', coupling[1], field[1])
    imag_part = jnp.einsum('yk,rkx->ryx', coupling[0], field[1]) + jnp.einsum('yk,rkx->ryx', coupling[1], field[0])
    return jnp.stack([real_part, imag_part])


def absorption(absorb_depth, column_count):
    column = jnp.arange(column_count, dtype=jnp.int32)
    distance = jnp.minimum(column, column_count - 1 - column).astype(jnp.float32)
    depth = absorb_depth.astype(jnp.float32)[:, None]
    ramp = jnp.maximum(depth - distance[None, :], 0.0) / depth
    return SIGMA_TOP * ramp * ramp


def operate(field, padded, slowness, absorb_depth):
    layer_count = field.shape[1]
    line_count = field.shape[3]
    column_count = field.shape[4]
    weights = (0.0, FACE, EDGE, CORNER)
    near = jnp.zeros(field.shape, jnp.float32)
    for depth_move in (-1, 0, 1):
        for line_move in (-1, 0, 1):
            for column_move in (-1, 0, 1):
                reach = abs(depth_move) + abs(line_move) + abs(column_move)
                if reach > 0:
                    near = near + weights[reach] * padded[:, 1 + depth_move:1 + depth_move + layer_count, :, 1 + line_move:1 + line_move + line_count, 1 + column_move:1 + column_move + column_count]
    damping = absorption(absorb_depth, column_count)
    wave_real = slowness[:, None, :, :]
    wave_imag = wave_real * damping[:, None, None, :]
    real_part = CENTER * field[0] - near[0] - (wave_real * field[0] - wave_imag * field[1])
    imag_part = CENTER * field[1] - near[1] - (wave_real * field[1] + wave_imag * field[0])
    return jnp.stack([real_part, imag_part])


def reference(rhs_field, slowness, absorb_depth, line_inverse, cross_inverse):
    def layer_step(prior, inputs):
        rhs_layer, coupling, index = inputs
        source = (rhs_layer + prior).astype(jnp.bfloat16)
        matrix = lax.dynamic_index_in_dim(line_inverse, index // LAY, 0, keepdims=False)
        mixed = complex_line(source.reshape(2, RHS * NY, NX), matrix).reshape(2, RHS, NY, NX)
        result = cross_mix(mixed, coupling)
        return result, result

    initial = jnp.zeros((2, RHS, NY, NX), jnp.float32)
    rhs_layers = jnp.moveaxis(rhs_field, 1, 0)
    indices = jnp.arange(NZ, dtype=jnp.int32)
    _, layers = lax.scan(layer_step, initial, (rhs_layers, cross_inverse, indices))
    solution = jnp.moveaxis(layers, 0, 1)
    padded = jnp.pad(solution, ((0, 0), (1, 1), (0, 0), (1, 1), (1, 1)))
    residual = rhs_field - operate(solution, padded, slowness, absorb_depth)
    return solution, residual
```

```python
import functools

import jax
import jax.numpy as jnp
from jax import lax
from jax.experimental import pallas as pl
from jax.experimental.pallas import tpu as pltpu
from jax.sharding import PartitionSpec as P

MESH = pl.DeviceIdType.MESH
SIGMA_TOP = 2.0
CENTER = 128.0 / 30.0
FACE = 14.0 / 30.0
EDGE = 3.0 / 30.0
CORNER = 1.0 / 30.0
PAD = 16
RHS = 2
BF = jnp.bfloat16


def kernel(
    n_s, n_c,
    rhs_ref, slow_ref, depth_ref, line_ref, cross_ref,
    sol_ref, res_ref,
    rhs_full, c_full, src, mixed, s_in, o_buf, ext, p_out, p_in,
    c_send, c_recv, r_send, r_recv, s_send, s_recv, y_send, e_send, e_recv, p_send, p_recv,
):
    rows, cols = slow_ref.shape[1], slow_ref.shape[2]
    height = rows * n_c
    group = n_c // RHS
    width = cols // group
    chunk = min(128, height)
    chunks = height // chunk
    sec = lax.axis_index("sec")
    p = lax.axis_index("cross")
    r = p // group
    h = p % group
    odd = sec % 2

    def remote(source, target, send, recv, where):
        return pltpu.make_async_remote_copy(
            src_ref=source, dst_ref=target, send_sem=send, recv_sem=recv,
            device_id=where, device_id_type=MESH,
        )

    def at_sec(s):
        return {"sec": s, "cross": p}

    def at_cross(q):
        return {"sec": sec, "cross": q}

    barrier = pltpu.get_barrier_semaphore()
    for d in range(1, n_c):
        pl.semaphore_signal(barrier, inc=1, device_id=at_cross((p + d) % n_c), device_id_type=MESH)

    @pl.when(sec > 0)
    def _():
        pl.semaphore_signal(barrier, inc=1, device_id=at_sec(sec - 1), device_id_type=MESH)

    @pl.when(sec < n_s - 1)
    def _():
        pl.semaphore_signal(barrier, inc=1, device_id=at_sec(sec + 1), device_id_type=MESH)

    def block(q):
        return pl.ds(pl.multiple_of(q * rows, rows), rows)

    for b in range(RHS):
        for c in range(2):
            rhs_full[b, c, block(p), :] = rhs_ref[c, 0, b].astype(BF)
    for c in range(2):
        c_full[c, block(p), :] = cross_ref[0, c]
    zeros_pad = jnp.zeros((PAD, width), BF)
    for j in range(group):
        for c in range(2):
            o_buf[j, c, 0:PAD, :] = zeros_pad
            o_buf[j, c, PAD + height : PAD + height + PAD, :] = zeros_pad

    pl.semaphore_wait(barrier, n_c - 1 + jnp.minimum(sec, 1) + jnp.minimum(n_s - 1 - sec, 1))

    def c_copy(q, way, to):
        return remote(c_full.at[:, block(q), :], c_full.at[:, block(q), :], c_send.at[way, q], c_recv.at[q], at_cross(to))

    def r_copy(b, q, way, to):
        return remote(rhs_full.at[b, :, block(q), :], rhs_full.at[b, :, block(q), :], r_send.at[b, way, q], r_recv.at[b, q], at_cross(to))

    def moves_right(b):
        return p < n_c - 1 if b == 1 else p + 1 < group

    def moves_left(b):
        return p > 0 if b == 0 else p - 1 >= group

    last = n_c - 1
    for t in range(n_c):
        a = p - t
        a0 = jnp.maximum(a, 0)
        z = p + t
        z0 = jnp.minimum(z, last)
        right = jnp.minimum(p + 1, last)
        left = jnp.maximum(p - 1, 0)
        for b in (1, 0):
            if t > 0:
                got = (a >= 0) if b == 1 else jnp.logical_and(a >= 0, p < group)

                @pl.when(got)
                def _():
                    r_copy(b, a0, 0, left).wait_recv()

            @pl.when(jnp.logical_and(a >= 0, moves_right(b)))
            def _():
                r_copy(b, a0, 0, right).start()

        for b in (0, 1):
            if t > 0:
                got = (z <= last) if b == 0 else jnp.logical_and(z <= last, p >= group)

                @pl.when(got)
                def _():
                    r_copy(b, z0, 1, right).wait_recv()

            @pl.when(jnp.logical_and(z <= last, moves_left(b)))
            def _():
                r_copy(b, z0, 1, left).start()

        if t > 0:
            @pl.when(a >= 0)
            def _():
                c_copy(a0, 0, left).wait_recv()

        @pl.when(jnp.logical_and(a >= 0, p < last))
        def _():
            c_copy(a0, 0, right).start()

        if t > 0:
            @pl.when(z <= last)
            def _():
                c_copy(z0, 1, right).wait_recv()

        @pl.when(jnp.logical_and(z <= last, p > 0))
        def _():
            c_copy(z0, 1, left).start()

    lo = odd * h
    hi = lo + (1 - odd) * group + odd

    def lines(i):
        return pl.ds(pl.multiple_of(i * chunk, chunk), chunk)

    def padded_lines(i):
        return pl.ds(pl.multiple_of(PAD + i * chunk, PAD), chunk)

    def part(j):
        return pl.ds(pl.multiple_of(j * width, width), width)

    def s_copy(i, j):
        return remote(
            o_buf.at[j, :, padded_lines(i), :], s_in.at[j, :, lines(i), :], s_send.at[i, j], s_recv.at[i, j],
            at_sec(jnp.minimum(sec + 1, n_s - 1)),
        )

    def y_copy(i, d):
        other = r * group + (h + d) % group
        return remote(
            s_in.at[h, :, lines(i), :], s_in.at[h, :, lines(i), :], y_send.at[i, d], s_recv.at[i, h], at_cross(other)
        )

    def s_wait(i, j):
        remote(
            o_buf.at[0, :, padded_lines(i), :], s_in.at[j, :, lines(i), :], s_send.at[i, 0], s_recv.at[i, j],
            at_sec(jnp.maximum(sec - 1, 0)),
        ).wait_recv()

    def times(left, w0, w1):
        one = jnp.dot(left, w0, preferred_element_type=jnp.float32)
        two = jnp.dot(left, w1, preferred_element_type=jnp.float32)
        half = left.shape[0] // 2
        return one[:half] - two[half:], two[:half] + one[half:]

    def take(i, _):
        @pl.when(sec > 0)
        def _():
            s_wait(i, h)

            @pl.when(odd == 0)
            def _():
                for d in range(1, group):
                    y_copy(i, d).start()

            for d in range(1, group):
                s_wait(i, (h + d) % group)

            for c in range(2):
                for j in range(group):
                    at = slice(j * width, (j + 1) * width)
                    src[c, :, at] = (
                        rhs_full[r, c, lines(i), at].astype(jnp.float32) + s_in[j, c, lines(i), :].astype(jnp.float32)
                    ).astype(BF)

        @pl.when(sec == 0)
        def _():
            for c in range(2):
                src[c] = rhs_full[r, c, lines(i), :]

        left = src[...].reshape(2 * chunk, cols)

        def of_part(j, _):
            re, im = times(left, line_ref[0, 0, :, part(j)], line_ref[0, 1, :, part(j)])
            mixed[j, 0, lines(i), :] = re.astype(BF)
            mixed[j, 1, lines(i), :] = im.astype(BF)
            return 0

        lax.fori_loop(lo, hi, of_part, 0)
        return 0

    lax.fori_loop(0, chunks, take, 0)

    def give(i, _):
        left = c_full[:, lines(i), :].reshape(2 * chunk, height)

        def of_part(j, _):
            re, im = times(left, mixed[j, 0], mixed[j, 1])
            o_buf[j, 0, padded_lines(i), :] = re.astype(BF)
            o_buf[j, 1, padded_lines(i), :] = im.astype(BF)

            @pl.when(sec < n_s - 1)
            def _():
                s_copy(i, j).start()

            return 0

        lax.fori_loop(lo, hi, of_part, 0)
        return 0

    lax.fori_loop(0, chunks, give, 0)

    tall = rows + 2 * PAD

    def own(q):
        return pl.ds(pl.multiple_of(q * rows, PAD), tall)

    def e_copy(d):
        q = (p + d) % n_c
        return remote(o_buf.at[h, :, own(q), :], ext.at[p], e_send.at[d], e_recv.at[p], at_cross(q))

    for d in range(1, n_c):
        e_copy(d).start()
    ext[p] = o_buf[h, :, own(p), :]
    for d in range(1, n_c):
        q = (p + d) % n_c
        remote(o_buf.at[h, :, own(q), :], ext.at[q], e_send.at[d], e_recv.at[q], at_cross(q)).wait_recv()

    column = lax.broadcasted_iota(jnp.int32, (rows, cols), 1)

    def sideways(v):
        before = jnp.where(column == 0, 0.0, pltpu.roll(v, 1, 1))
        after = jnp.where(column == cols - 1, 0.0, pltpu.roll(v, cols - 1, 1))
        return before + after

    for b in range(RHS):
        for c in range(2):
            f = jnp.concatenate([ext[b * group + j, c].astype(jnp.float32) for j in range(group)], axis=1)
            here = f[PAD : PAD + rows]
            updown = (pltpu.roll(f, 1, 0) + pltpu.roll(f, tall - 1, 0))[PAD : PAD + rows]
            faces = updown + sideways(here)
            corners = sideways(updown)
            sol_ref[c, 0, b] = here
            p_out[c, b] = (FACE * here + EDGE * faces + CORNER * corners).astype(BF)
            res_ref[c, 0, b] = rhs_ref[c, 0, b] - CENTER * here + (FACE * faces + EDGE * corners)

    def p_copy(way):
        to = jnp.maximum(sec - 1, 0) if way == 1 else jnp.minimum(sec + 1, n_s - 1)
        return remote(p_out, p_in.at[way], p_send.at[way], p_recv.at[way], at_sec(to))

    @pl.when(sec < n_s - 1)
    def _():
        p_copy(0).start()

    @pl.when(sec > 0)
    def _():
        p_copy(1).start()

    line = lax.broadcasted_iota(jnp.int32, (1, cols), 1)
    distance = jnp.minimum(line, cols - 1 - line).astype(jnp.float32)
    depth = jnp.full((1, cols), depth_ref[0], jnp.int32).astype(jnp.float32)
    ramp = jnp.maximum(depth - distance, 0.0) / depth
    damping = SIGMA_TOP * ramp * ramp
    wave_real = slow_ref[0]
    wave_imag = wave_real * damping
    for b in range(RHS):
        re, im = sol_ref[0, 0, b], sol_ref[1, 0, b]
        res_ref[0, 0, b] += wave_real * re - wave_imag * im
        res_ref[1, 0, b] += wave_real * im + wave_imag * re

    def neighbour(way):
        p_copy(way).wait_recv()
        for b in range(RHS):
            for c in range(2):
                res_ref[c, 0, b] += p_in[way, c, b].astype(jnp.float32)

    @pl.when(sec > 0)
    def _():
        neighbour(0)

    @pl.when(sec < n_s - 1)
    def _():
        neighbour(1)

    for t in range(n_c):
        a = p - t
        a0 = jnp.maximum(a, 0)
        z = p + t
        z0 = jnp.minimum(z, last)
        right = jnp.minimum(p + 1, last)
        left = jnp.maximum(p - 1, 0)
        for b in range(RHS):
            @pl.when(jnp.logical_and(a >= 0, moves_right(b)))
            def _():
                r_copy(b, a0, 0, right).wait_send()

            @pl.when(jnp.logical_and(z <= last, moves_left(b)))
            def _():
                r_copy(b, z0, 1, left).wait_send()

        @pl.when(jnp.logical_and(a >= 0, p < last))
        def _():
            c_copy(a0, 0, right).wait_send()

        @pl.when(jnp.logical_and(z <= last, p > 0))
        def _():
            c_copy(z0, 1, left).wait_send()

    def sent(i, _):
        @pl.when(sec < n_s - 1)
        def _():
            def one(j, _):
                s_copy(i, j).wait_send()
                return 0

            lax.fori_loop(lo, hi, one, 0)

        @pl.when(jnp.logical_and(sec > 0, odd == 0))
        def _():
            for d in range(1, group):
                y_copy(i, d).wait_send()

        return 0

    lax.fori_loop(0, chunks, sent, 0)
    for d in range(1, n_c):
        e_copy(d).wait_send()

    @pl.when(sec < n_s - 1)
    def _():
        p_copy(0).wait_send()

    @pl.when(sec > 0)
    def _():
        p_copy(1).wait_send()


def per_device(n_s, n_c, rhs_field, slowness, absorb_depth, line_inverse, cross_inverse):
    rows, cols = slowness.shape[1:]
    height = rows * n_c
    group = n_c // RHS
    width = cols // group
    chunk = min(128, height)
    chunks = height // chunk
    vmem = pl.BlockSpec(memory_space=pltpu.VMEM)
    dma = pltpu.SemaphoreType.DMA
    out = jax.ShapeDtypeStruct(rhs_field.shape, jnp.float32)
    return pl.pallas_call(
        functools.partial(kernel, n_s, n_c),
        out_shape=(out, out),
        in_specs=[vmem, vmem, pl.BlockSpec(memory_space=pltpu.SMEM), vmem, vmem],
        out_specs=(vmem, vmem),
        scratch_shapes=[
            pltpu.VMEM((RHS, 2, height, cols), BF),
            pltpu.VMEM((2, height, height), BF),
            pltpu.VMEM((2, chunk, cols), BF),
            pltpu.VMEM((group, 2, height, width), BF),
            pltpu.VMEM((group, 2, height, width), BF),
            pltpu.VMEM((group, 2, height + 2 * PAD, width), BF),
            pltpu.VMEM((n_c, 2, rows + 2 * PAD, width), BF),
            pltpu.VMEM((2, RHS, rows, cols), BF),
            pltpu.VMEM((2, 2, RHS, rows, cols), BF),
            dma((2, n_c)), dma((n_c,)),
            dma((RHS, 2, n_c)), dma((RHS, n_c)),
            dma((chunks, group)), dma((chunks, group)), dma((chunks, group)),
            dma((n_c,)), dma((n_c,)),
            dma((2,)), dma((2,)),
        ],
        compiler_params=pltpu.CompilerParams(
            collective_id=0, has_side_effects=True, vmem_limit_bytes=56 * 1024 * 1024
        ),
        name="sweep",
    )(rhs_field, slowness, absorb_depth, line_inverse, cross_inverse)


def solution(mesh):
    field = P(None, "sec", None, "cross", None)
    return jax.shard_map(
        functools.partial(per_device, mesh.shape["sec"], mesh.shape["cross"]),
        mesh=mesh,
        in_specs=(
            field,
            P("sec", "cross", None),
            P("sec"),
            P("sec", None, None, None),
            P("sec", None, "cross", None),
        ),
        out_specs=(field, field),
        check_vma=False,
    )
```

```python
import functools

import jax
import jax.numpy as jnp
from jax import lax
from jax.experimental import pallas as pl
from jax.experimental.pallas import tpu as pltpu
from jax.sharding import PartitionSpec as P

MESH = pl.DeviceIdType.MESH
SIGMA_TOP = 2.0
CENTER = 128.0 / 30.0
FACE = 14.0 / 30.0
EDGE = 3.0 / 30.0
CORNER = 1.0 / 30.0
PAD = 16
RHS = 2
BF = jnp.bfloat16


def kernel(
    n_s, n_c,
    rhs_ref, slow_ref, depth_ref, line_ref, cross_ref,
    sol_ref, res_ref,
    rhs_full, c_full, r_in, c_in, l_in, weight, direct, src, mixed, s_in, o_buf, ext, p_out, p_in,
    c_send, c_recv, r_send, r_recv, f_send, f_recv, l_send, l_recv,
    s_send, s_recv, y_send, d_send, e_send, e_recv, p_send, p_recv,
):
    rows, cols = slow_ref.shape[1], slow_ref.shape[2]
    height = rows * n_c
    group = n_c // RHS
    width = cols // group
    chunk = min(128, height)
    chunks = height // chunk
    sec = lax.axis_index("sec")
    p = lax.axis_index("cross")
    r = p // group
    h = p % group
    odd = sec % 2

    def remote(source, target, send, recv, where):
        return pltpu.make_async_remote_copy(
            src_ref=source, dst_ref=target, send_sem=send, recv_sem=recv,
            device_id=where, device_id_type=MESH,
        )

    def at_sec(s):
        return {"sec": s, "cross": p}

    def at_cross(q):
        return {"sec": sec, "cross": q}

    barrier = pltpu.get_barrier_semaphore()
    for d in range(1, n_c):
        pl.semaphore_signal(barrier, inc=1, device_id=at_cross((p + d) % n_c), device_id_type=MESH)

    @pl.when(sec > 0)
    def _():
        pl.semaphore_signal(barrier, inc=1, device_id=at_sec(sec - 1), device_id_type=MESH)

    @pl.when(sec < n_s - 1)
    def _():
        pl.semaphore_signal(barrier, inc=1, device_id=at_sec(sec + 1), device_id_type=MESH)

    @pl.when(jnp.logical_and(odd == 1, sec >= 2))
    def _():
        pl.semaphore_signal(barrier, inc=1, device_id=at_sec(sec - 2), device_id_type=MESH)

    @pl.when(jnp.logical_and(odd == 1, sec <= n_s - 3))
    def _():
        pl.semaphore_signal(barrier, inc=1, device_id=at_sec(sec + 2), device_id_type=MESH)

    def block(q):
        return pl.ds(pl.multiple_of(q * rows, rows), rows)

    for b in range(RHS):
        for c in range(2):
            rhs_full[b, c, block(p), :] = rhs_ref[c, 0, b].astype(BF)
    for c in range(2):
        c_full[c, block(p), :] = cross_ref[0, c]
    zeros_pad = jnp.zeros((PAD, width), BF)
    for j in range(group):
        for c in range(2):
            o_buf[j, c, 0:PAD, :] = zeros_pad
            o_buf[j, c, PAD + height : PAD + height + PAD, :] = zeros_pad

    nearest = jnp.minimum(sec, 1) + jnp.minimum(n_s - 1 - sec, 1)
    second = jnp.minimum(sec // 2, 1) + jnp.minimum((n_s - 1 - sec) // 2, 1)
    pl.semaphore_wait(barrier, n_c - 1 + nearest + odd * second)

    def c_copy(q, way, to):
        return remote(c_full.at[:, block(q), :], c_full.at[:, block(q), :], c_send.at[way, q], c_recv.at[q], at_cross(to))

    def r_copy(b, q, way, to):
        return remote(rhs_full.at[b, :, block(q), :], rhs_full.at[b, :, block(q), :], r_send.at[b, way, q], r_recv.at[b, q], at_cross(to))

    partner = sec + 1 - 2 * odd

    def f_copy(kind, q):
        source, target = (rhs_full.at[r], r_in) if kind == 0 else (c_full, c_in)
        return remote(
            source.at[:, block(q), :], target.at[:, block(q), :], f_send.at[kind, q], f_recv.at[kind, q], at_sec(partner)
        )

    def l_copy():
        return remote(line_ref.at[0], l_in, l_send, l_recv, at_sec(partner))

    def times(left, w0, w1):
        one = jnp.dot(left, w0, preferred_element_type=jnp.float32)
        two = jnp.dot(left, w1, preferred_element_type=jnp.float32)
        half = left.shape[0] // 2
        return one[:half] - two[half:], two[:half] + one[half:]

    def lines(i):
        return pl.ds(pl.multiple_of(i * chunk, chunk), chunk)

    def part(j):
        return pl.ds(pl.multiple_of(j * width, width), width)

    span = min(128, cols)

    def weights():
        @pl.when(odd == 0)
        def _():
            for c in range(2):
                weight[c] = line_ref[0, c, :, part(h)]

        @pl.when(odd == 1)
        def _():
            l_copy().wait_recv()

            def rows_of(i, _):
                at = pl.ds(pl.multiple_of(i * span, span), span)
                re, im = times(
                    l_in[:, at, :].reshape(2 * span, cols), line_ref[0, 0, :, part(h)], line_ref[0, 1, :, part(h)]
                )
                weight[0, at, :] = re.astype(BF)
                weight[1, at, :] = im.astype(BF)
                return 0

            lax.fori_loop(0, cols // span, rows_of, 0)

    @pl.when(odd == 0)
    def _():
        l_copy().start()

    def moves_right(b):
        return p < n_c - 1 if b == 1 else p + 1 < group

    def moves_left(b):
        return p > 0 if b == 0 else p - 1 >= group

    last = n_c - 1
    for t in range(n_c):
        a = p - t
        a0 = jnp.maximum(a, 0)
        z = p + t
        z0 = jnp.minimum(z, last)
        right = jnp.minimum(p + 1, last)
        left = jnp.maximum(p - 1, 0)
        for b in (1, 0):
            if t > 0:
                got = (a >= 0) if b == 1 else jnp.logical_and(a >= 0, p < group)

                @pl.when(got)
                def _():
                    r_copy(b, a0, 0, left).wait_recv()

                @pl.when(jnp.logical_and(got, jnp.logical_and(odd == 0, r == b)))
                def _():
                    f_copy(0, a0).start()

            @pl.when(jnp.logical_and(a >= 0, moves_right(b)))
            def _():
                r_copy(b, a0, 0, right).start()

        for b in (0, 1):
            if t > 0:
                got = (z <= last) if b == 0 else jnp.logical_and(z <= last, p >= group)

                @pl.when(got)
                def _():
                    r_copy(b, z0, 1, right).wait_recv()

                @pl.when(jnp.logical_and(got, jnp.logical_and(odd == 0, r == b)))
                def _():
                    f_copy(0, z0).start()

            @pl.when(jnp.logical_and(z <= last, moves_left(b)))
            def _():
                r_copy(b, z0, 1, left).start()

        if t > 0:
            @pl.when(a >= 0)
            def _():
                c_copy(a0, 0, left).wait_recv()

            @pl.when(jnp.logical_and(a >= 0, odd == 0))
            def _():
                f_copy(1, a0).start()

        @pl.when(jnp.logical_and(a >= 0, p < last))
        def _():
            c_copy(a0, 0, right).start()

        if t > 0:
            @pl.when(z <= last)
            def _():
                c_copy(z0, 1, right).wait_recv()

            @pl.when(jnp.logical_and(z <= last, odd == 0))
            def _():
                f_copy(1, z0).start()

        @pl.when(jnp.logical_and(z <= last, p > 0))
        def _():
            c_copy(z0, 1, left).start()

        if t == 0:
            @pl.when(odd == 0)
            def _():
                f_copy(0, p).start()
                f_copy(1, p).start()

            weights()

    def padded_lines(i):
        return pl.ds(pl.multiple_of(PAD + i * chunk, PAD), chunk)

    def s_copy(i):
        return remote(
            o_buf.at[h, :, padded_lines(i), :], s_in.at[h, :, lines(i), :], s_send.at[i], s_recv.at[i, h],
            at_sec(jnp.minimum(sec + 2, n_s - 1)),
        )

    def y_copy(i, d):
        other = r * group + (h + d) % group
        return remote(
            s_in.at[h, :, lines(i), :], s_in.at[h, :, lines(i), :], y_send.at[i, d], s_recv.at[i, h], at_cross(other)
        )

    def d_copy(i, j):
        return remote(
            s_in.at[j, :, lines(i), :], s_in.at[j, :, lines(i), :], d_send.at[i, j], s_recv.at[i, j], at_sec(partner)
        )

    @pl.when(odd == 1)
    def _():
        def own_lines(i, _):
            re, im = times(
                rhs_full[r, :, lines(i), :].reshape(2 * chunk, cols), line_ref[0, 0, :, part(h)], line_ref[0, 1, :, part(h)]
            )
            direct[0, lines(i), :] = re
            direct[1, lines(i), :] = im
            return 0

        lax.fori_loop(0, chunks, own_lines, 0)
        for q in range(n_c):
            f_copy(0, q).wait_recv()

    @pl.when(odd == 0)
    def _():
        r_in[...] = rhs_full[r]

    def take(i, _):
        @pl.when(sec >= 2)
        def _():
            d_copy(i, h).wait_recv()

            @pl.when(odd == 1)
            def _():
                for d in range(1, group):
                    y_copy(i, d).start()
                d_copy(i, h).start()

            for d in range(1, group):
                j = (h + d) % group
                d_copy(i, j).wait_recv()

                @pl.when(odd == 1)
                def _():
                    d_copy(i, j).start()

            for c in range(2):
                for j in range(group):
                    at = slice(j * width, (j + 1) * width)
                    src[c, :, at] = (
                        r_in[c, lines(i), at].astype(jnp.float32) + s_in[j, c, lines(i), :].astype(jnp.float32)
                    ).astype(BF)

        @pl.when(sec < 2)
        def _():
            src[...] = r_in[:, lines(i), :]

        re, im = times(src[...].reshape(2 * chunk, cols), weight[0], weight[1])
        mixed[odd, 0, lines(i), :] = re.astype(BF)
        mixed[odd, 1, lines(i), :] = im.astype(BF)
        return 0

    lax.fori_loop(0, chunks, take, 0)

    @pl.when(odd == 1)
    def _():
        for q in range(n_c):
            f_copy(1, q).wait_recv()

        def even_layer(i, _):
            re, im = times(c_in[:, lines(i), :].reshape(2 * chunk, height), mixed[1, 0], mixed[1, 1])
            mixed[0, 0, lines(i), :] = (direct[0, lines(i), :] + re).astype(BF)
            mixed[0, 1, lines(i), :] = (direct[1, lines(i), :] + im).astype(BF)
            return 0

        lax.fori_loop(0, chunks, even_layer, 0)

    hands_on = jnp.logical_and(odd == 1, sec <= n_s - 3)

    def give(i, _):
        re, im = times(c_full[:, lines(i), :].reshape(2 * chunk, height), mixed[0, 0], mixed[0, 1])
        o_buf[h, 0, padded_lines(i), :] = re.astype(BF)
        o_buf[h, 1, padded_lines(i), :] = im.astype(BF)

        @pl.when(hands_on)
        def _():
            s_copy(i).start()

        return 0

    lax.fori_loop(0, chunks, give, 0)

    tall = rows + 2 * PAD

    def own(q):
        return pl.ds(pl.multiple_of(q * rows, PAD), tall)

    def e_copy(d):
        q = (p + d) % n_c
        return remote(o_buf.at[h, :, own(q), :], ext.at[p], e_send.at[d], e_recv.at[p], at_cross(q))

    for d in range(1, n_c):
        e_copy(d).start()
    ext[p] = o_buf[h, :, own(p), :]
    for d in range(1, n_c):
        q = (p + d) % n_c
        remote(o_buf.at[h, :, own(q), :], ext.at[q], e_send.at[d], e_recv.at[q], at_cross(q)).wait_recv()

    column = lax.broadcasted_iota(jnp.int32, (rows, cols), 1)

    def sideways(v):
        before = jnp.where(column == 0, 0.0, pltpu.roll(v, 1, 1))
        after = jnp.where(column == cols - 1, 0.0, pltpu.roll(v, cols - 1, 1))
        return before + after

    for b in range(RHS):
        for c in range(2):
            f = jnp.concatenate([ext[b * group + j, c].astype(jnp.float32) for j in range(group)], axis=1)
            here = f[PAD : PAD + rows]
            updown = (pltpu.roll(f, 1, 0) + pltpu.roll(f, tall - 1, 0))[PAD : PAD + rows]
            faces = updown + sideways(here)
            corners = sideways(updown)
            sol_ref[c, 0, b] = here
            p_out[c, b] = (FACE * here + EDGE * faces + CORNER * corners).astype(BF)
            res_ref[c, 0, b] = rhs_ref[c, 0, b] - CENTER * here + (FACE * faces + EDGE * corners)

    def p_copy(way):
        to = jnp.maximum(sec - 1, 0) if way == 1 else jnp.minimum(sec + 1, n_s - 1)
        return remote(p_out, p_in.at[way], p_send.at[way], p_recv.at[way], at_sec(to))

    @pl.when(sec < n_s - 1)
    def _():
        p_copy(0).start()

    @pl.when(sec > 0)
    def _():
        p_copy(1).start()

    line = lax.broadcasted_iota(jnp.int32, (1, cols), 1)
    distance = jnp.minimum(line, cols - 1 - line).astype(jnp.float32)
    depth = jnp.full((1, cols), depth_ref[0], jnp.int32).astype(jnp.float32)
    ramp = jnp.maximum(depth - distance, 0.0) / depth
    damping = SIGMA_TOP * ramp * ramp
    wave_real = slow_ref[0]
    wave_imag = wave_real * damping
    for b in range(RHS):
        re, im = sol_ref[0, 0, b], sol_ref[1, 0, b]
        res_ref[0, 0, b] += wave_real * re - wave_imag * im
        res_ref[1, 0, b] += wave_real * im + wave_imag * re

    def neighbour(way):
        p_copy(way).wait_recv()
        for b in range(RHS):
            for c in range(2):
                res_ref[c, 0, b] += p_in[way, c, b].astype(jnp.float32)

    @pl.when(sec > 0)
    def _():
        neighbour(0)

    @pl.when(sec < n_s - 1)
    def _():
        neighbour(1)

    for t in range(n_c):
        a = p - t
        a0 = jnp.maximum(a, 0)
        z = p + t
        z0 = jnp.minimum(z, last)
        right = jnp.minimum(p + 1, last)
        left = jnp.maximum(p - 1, 0)
        for b in range(RHS):
            @pl.when(jnp.logical_and(a >= 0, moves_right(b)))
            def _():
                r_copy(b, a0, 0, right).wait_send()

            @pl.when(jnp.logical_and(z <= last, moves_left(b)))
            def _():
                r_copy(b, z0, 1, left).wait_send()

        @pl.when(jnp.logical_and(a >= 0, p < last))
        def _():
            c_copy(a0, 0, right).wait_send()

        @pl.when(jnp.logical_and(z <= last, p > 0))
        def _():
            c_copy(z0, 1, left).wait_send()

    def sent(i, _):
        @pl.when(hands_on)
        def _():
            s_copy(i).wait_send()

        @pl.when(jnp.logical_and(sec >= 2, odd == 1))
        def _():
            for d in range(1, group):
                y_copy(i, d).wait_send()
            for j in range(group):
                d_copy(i, j).wait_send()

        return 0

    @pl.when(odd == 0)
    def _():
        l_copy().wait_send()
        for q in range(n_c):
            f_copy(0, q).wait_send()
            f_copy(1, q).wait_send()

    lax.fori_loop(0, chunks, sent, 0)
    for d in range(1, n_c):
        e_copy(d).wait_send()

    @pl.when(sec < n_s - 1)
    def _():
        p_copy(0).wait_send()

    @pl.when(sec > 0)
    def _():
        p_copy(1).wait_send()


def per_device(n_s, n_c, rhs_field, slowness, absorb_depth, line_inverse, cross_inverse):
    rows, cols = slowness.shape[1:]
    height = rows * n_c
    group = n_c // RHS
    width = cols // group
    chunk = min(128, height)
    chunks = height // chunk
    vmem = pl.BlockSpec(memory_space=pltpu.VMEM)
    dma = pltpu.SemaphoreType.DMA
    out = jax.ShapeDtypeStruct(rhs_field.shape, jnp.float32)
    return pl.pallas_call(
        functools.partial(kernel, n_s, n_c),
        out_shape=(out, out),
        in_specs=[vmem, vmem, pl.BlockSpec(memory_space=pltpu.SMEM), vmem, vmem],
        out_specs=(vmem, vmem),
        scratch_shapes=[
            pltpu.VMEM((RHS, 2, height, cols), BF),
            pltpu.VMEM((2, height, height), BF),
            pltpu.VMEM((2, height, cols), BF),
            pltpu.VMEM((2, height, height), BF),
            pltpu.VMEM((2, cols, cols), BF),
            pltpu.VMEM((2, cols, width), BF),
            pltpu.VMEM((2, height, width), jnp.float32),
            pltpu.VMEM((2, chunk, cols), BF),
            pltpu.VMEM((2, 2, height, width), BF),
            pltpu.VMEM((group, 2, height, width), BF),
            pltpu.VMEM((group, 2, height + 2 * PAD, width), BF),
            pltpu.VMEM((n_c, 2, rows + 2 * PAD, width), BF),
            pltpu.VMEM((2, RHS, rows, cols), BF),
            pltpu.VMEM((2, 2, RHS, rows, cols), BF),
            dma((2, n_c)), dma((n_c,)),
            dma((RHS, 2, n_c)), dma((RHS, n_c)),
            dma((2, n_c)), dma((2, n_c)), dma, dma,
            dma((chunks,)), dma((chunks, group)), dma((chunks, group)), dma((chunks, group)),
            dma((n_c,)), dma((n_c,)),
            dma((2,)), dma((2,)),
        ],
        compiler_params=pltpu.CompilerParams(
            collective_id=0, has_side_effects=True, vmem_limit_bytes=56 * 1024 * 1024
        ),
        name="sweep",
    )(rhs_field, slowness, absorb_depth, line_inverse, cross_inverse)


def solution(mesh):
    field = P(None, "sec", None, "cross", None)
    return jax.shard_map(
        functools.partial(per_device, mesh.shape["sec"], mesh.shape["cross"]),
        mesh=mesh,
        in_specs=(
            field,
            P("sec", "cross", None),
            P("sec"),
            P("sec", None, None, None),
            P("sec", None, "cross", None),
        ),
        out_specs=(field, field),
        check_vma=False,
    )
```

```python
import functools

import jax
import jax.numpy as jnp
from jax import lax
from jax.experimental import pallas as pl
from jax.experimental.pallas import tpu as pltpu
from jax.sharding import PartitionSpec as P

MESH = pl.DeviceIdType.MESH
SIGMA_TOP = 2.0
CENTER = 128.0 / 30.0
FACE = 14.0 / 30.0
EDGE = 3.0 / 30.0
CORNER = 1.0 / 30.0
PAD = 16
RHS = 2
BF = jnp.bfloat16


def kernel(
    n_s, n_c,
    rhs_ref, slow_ref, depth_ref, line_ref, cross_ref,
    sol_ref, res_ref,
    rhs_full, c_full, r_in, c_in, l_in, weight, direct, src, both, mixed, s_in, o_buf, ext, p_out, p_in,
    c_send, c_recv, r_send, r_recv, f_send, f_recv, l_send, l_recv,
    s_send, s_recv, y_send, d_send, e_send, e_recv, p_send, p_recv,
):
    rows, cols = slow_ref.shape[1], slow_ref.shape[2]
    height = rows * n_c
    group = n_c // RHS
    width = cols // group
    chunk = min(128, height)
    chunks = height // chunk
    sec = lax.axis_index("sec")
    p = lax.axis_index("cross")
    r = p // group
    h = p % group
    odd = sec % 2

    def remote(source, target, send, recv, where):
        return pltpu.make_async_remote_copy(
            src_ref=source, dst_ref=target, send_sem=send, recv_sem=recv,
            device_id=where, device_id_type=MESH,
        )

    def at_sec(s):
        return {"sec": s, "cross": p}

    def at_cross(q):
        return {"sec": sec, "cross": q}

    barrier = pltpu.get_barrier_semaphore()
    for d in range(1, n_c):
        pl.semaphore_signal(barrier, inc=1, device_id=at_cross((p + d) % n_c), device_id_type=MESH)

    @pl.when(sec > 0)
    def _():
        pl.semaphore_signal(barrier, inc=1, device_id=at_sec(sec - 1), device_id_type=MESH)

    @pl.when(sec < n_s - 1)
    def _():
        pl.semaphore_signal(barrier, inc=1, device_id=at_sec(sec + 1), device_id_type=MESH)

    @pl.when(jnp.logical_and(odd == 1, sec >= 2))
    def _():
        pl.semaphore_signal(barrier, inc=1, device_id=at_sec(sec - 2), device_id_type=MESH)

    @pl.when(jnp.logical_and(odd == 1, sec <= n_s - 3))
    def _():
        pl.semaphore_signal(barrier, inc=1, device_id=at_sec(sec + 2), device_id_type=MESH)

    def block(q):
        return pl.ds(pl.multiple_of(q * rows, rows), rows)

    for b in range(RHS):
        for c in range(2):
            rhs_full[b, c, block(p), :] = rhs_ref[c, 0, b].astype(BF)
    for c in range(2):
        c_full[c, block(p), :] = cross_ref[0, c]
    zeros_pad = jnp.zeros((PAD, width), BF)
    for j in range(group):
        for c in range(2):
            o_buf[j, c, 0:PAD, :] = zeros_pad
            o_buf[j, c, PAD + height : PAD + height + PAD, :] = zeros_pad

    nearest = jnp.minimum(sec, 1) + jnp.minimum(n_s - 1 - sec, 1)
    second = jnp.minimum(sec // 2, 1) + jnp.minimum((n_s - 1 - sec) // 2, 1)
    pl.semaphore_wait(barrier, n_c - 1 + nearest + odd * second)

    def c_copy(q, way, to):
        return remote(c_full.at[:, block(q), :], c_full.at[:, block(q), :], c_send.at[way, q], c_recv.at[q], at_cross(to))

    def r_copy(b, q, way, to):
        return remote(rhs_full.at[b, :, block(q), :], rhs_full.at[b, :, block(q), :], r_send.at[b, way, q], r_recv.at[b, q], at_cross(to))

    partner = sec + 1 - 2 * odd

    def f_copy(kind, q):
        source, target = (rhs_full.at[r], r_in) if kind == 0 else (c_full, c_in)
        return remote(
            source.at[:, block(q), :], target.at[:, block(q), :], f_send.at[kind, q], f_recv.at[kind, q], at_sec(partner)
        )

    def l_copy():
        return remote(line_ref.at[0], l_in, l_send, l_recv, at_sec(partner))

    def times(left, w0, w1):
        one = jnp.dot(left, w0, preferred_element_type=jnp.float32)
        two = jnp.dot(left, w1, preferred_element_type=jnp.float32)
        half = left.shape[0] // 2
        return one[:half] - two[half:], two[:half] + one[half:]

    def lines(i):
        return pl.ds(pl.multiple_of(i * chunk, chunk), chunk)

    def part(j):
        return pl.ds(pl.multiple_of(j * width, width), width)

    span = min(128, cols)

    def weights():
        @pl.when(odd == 0)
        def _():
            for c in range(2):
                weight[c] = line_ref[0, c, :, part(h)]

        @pl.when(odd == 1)
        def _():
            l_copy().wait_recv()

            def rows_of(i, _):
                at = pl.ds(pl.multiple_of(i * span, span), span)
                re, im = times(
                    l_in[:, at, :].reshape(2 * span, cols), line_ref[0, 0, :, part(h)], line_ref[0, 1, :, part(h)]
                )
                weight[0, at, :] = re.astype(BF)
                weight[1, at, :] = im.astype(BF)
                return 0

            lax.fori_loop(0, cols // span, rows_of, 0)

    @pl.when(odd == 0)
    def _():
        l_copy().start()

    def moves_right(b):
        return p < n_c - 1 if b == 1 else p + 1 < group

    def moves_left(b):
        return p > 0 if b == 0 else p - 1 >= group

    last = n_c - 1
    right = jnp.minimum(p + 1, last)
    left = jnp.maximum(p - 1, 0)

    def places(t):
        return p - t >= 0, jnp.maximum(p - t, 0), p + t <= last, jnp.minimum(p + t, last)

    def forward(kind, q, got):
        @pl.when(jnp.logical_and(got, odd == 0))
        def _():
            f_copy(kind, q).start()

    def relay_r(t):
        is_a, a, is_z, z = places(t)
        for b in (1, 0):
            if t > 0:
                got = is_a if b == 1 else jnp.logical_and(is_a, p < group)

                @pl.when(got)
                def _():
                    r_copy(b, a, 0, left).wait_recv()

                forward(0, a, jnp.logical_and(got, r == b))

            @pl.when(jnp.logical_and(is_a, moves_right(b)))
            def _():
                r_copy(b, a, 0, right).start()

        for b in (0, 1):
            if t > 0:
                got = is_z if b == 0 else jnp.logical_and(is_z, p >= group)

                @pl.when(got)
                def _():
                    r_copy(b, z, 1, right).wait_recv()

                forward(0, z, jnp.logical_and(got, r == b))

            @pl.when(jnp.logical_and(is_z, moves_left(b)))
            def _():
                r_copy(b, z, 1, left).start()

    def relay_c(t):
        is_a, a, is_z, z = places(t)
        if t > 0:
            @pl.when(is_a)
            def _():
                c_copy(a, 0, left).wait_recv()

            forward(1, a, is_a)

        @pl.when(jnp.logical_and(is_a, p < last))
        def _():
            c_copy(a, 0, right).start()

        if t > 0:
            @pl.when(is_z)
            def _():
                c_copy(z, 1, right).wait_recv()

            forward(1, z, is_z)

        @pl.when(jnp.logical_and(is_z, p > 0))
        def _():
            c_copy(z, 1, left).start()

    tall_chunk = min(256, height)

    def tall_lines(i):
        return pl.ds(pl.multiple_of(i * tall_chunk, tall_chunk), tall_chunk)

    def line_products():
        @pl.when(odd == 1)
        def _():
            for q in range(n_c):
                f_copy(0, q).wait_recv()

        def some(i, _):
            @pl.when(odd == 1)
            def _():
                re, im = times(
                    rhs_full[r, :, tall_lines(i), :].reshape(2 * tall_chunk, cols),
                    line_ref[0, 0, :, part(h)], line_ref[0, 1, :, part(h)],
                )
                direct[0, tall_lines(i), :] = re
                direct[1, tall_lines(i), :] = im
                src[:, tall_lines(i), :] = r_in[:, tall_lines(i), :]

            @pl.when(odd == 0)
            def _():
                src[:, tall_lines(i), :] = rhs_full[r, :, tall_lines(i), :]

            re, im = times(src[:, tall_lines(i), :].reshape(2 * tall_chunk, cols), weight[0], weight[1])
            mixed[odd, 0, tall_lines(i), :] = re.astype(BF)
            mixed[odd, 1, tall_lines(i), :] = im.astype(BF)
            return 0

        lax.fori_loop(0, height // tall_chunk, some, 0)

    relay_r(0)
    relay_c(0)
    forward(0, p, p >= 0)
    forward(1, p, p >= 0)
    weights()
    for t in range(1, n_c):
        relay_r(t)
    relay_c(1)
    line_products()
    for t in range(2, n_c):
        relay_c(t)

    def padded_lines(i):
        return pl.ds(pl.multiple_of(PAD + i * chunk, PAD), chunk)

    def s_copy(i):
        return remote(
            o_buf.at[h, :, padded_lines(i), :], s_in.at[h, :, lines(i), :], s_send.at[i], s_recv.at[i, h],
            at_sec(jnp.minimum(sec + 2, n_s - 1)),
        )

    def y_copy(i, d):
        other = r * group + (h + d) % group
        return remote(
            s_in.at[h, :, lines(i), :], s_in.at[h, :, lines(i), :], y_send.at[i, d], s_recv.at[i, h], at_cross(other)
        )

    def d_copy(i, j):
        return remote(
            s_in.at[j, :, lines(i), :], s_in.at[j, :, lines(i), :], d_send.at[i, j], s_recv.at[i, j], at_sec(partner)
        )

    @pl.when(odd == 1)
    def _():
        for q in range(n_c):
            f_copy(1, q).wait_recv()

        def even_layer(i, _):
            re, im = times(c_in[:, tall_lines(i), :].reshape(2 * tall_chunk, height), mixed[1, 0], mixed[1, 1])
            mixed[0, 0, tall_lines(i), :] = (direct[0, tall_lines(i), :] + re).astype(BF)
            mixed[0, 1, tall_lines(i), :] = (direct[1, tall_lines(i), :] + im).astype(BF)
            return 0

        lax.fori_loop(0, height // tall_chunk, even_layer, 0)

    hands_on = jnp.logical_and(odd == 1, sec <= n_s - 3)

    def put(i, re, im):
        o_buf[h, 0, padded_lines(i), :] = re.astype(BF)
        o_buf[h, 1, padded_lines(i), :] = im.astype(BF)

        @pl.when(hands_on)
        def _():
            s_copy(i).start()

    def alone(i, _):
        re, im = times(c_full[:, lines(i), :].reshape(2 * chunk, height), mixed[0, 0], mixed[0, 1])

        @pl.when(sec < 2)
        def _():
            put(i, re, im)

        @pl.when(sec >= 2)
        def _():
            direct[0, lines(i), :] = re
            direct[1, lines(i), :] = im

            @pl.when(odd == 0)
            def _():
                both[:, lines(i), :] = c_full[:, lines(i), :]

            @pl.when(odd == 1)
            def _():
                re, im = times(c_full[:, lines(i), :].reshape(2 * chunk, height), c_in[0], c_in[1])
                both[0, lines(i), :] = re.astype(BF)
                both[1, lines(i), :] = im.astype(BF)

        return 0

    lax.fori_loop(0, chunks, alone, 0)

    @pl.when(sec >= 2)
    def _():
        def take(i, _):
            d_copy(i, h).wait_recv()

            @pl.when(odd == 1)
            def _():
                for d in range(1, group):
                    y_copy(i, d).start()
                d_copy(i, h).start()

            for d in range(1, group):
                j = (h + d) % group
                d_copy(i, j).wait_recv()

                @pl.when(odd == 1)
                def _():
                    d_copy(i, j).start()

            for c in range(2):
                for j in range(group):
                    src[c, lines(i), j * width : (j + 1) * width] = s_in[j, c, lines(i), :]
            re, im = times(src[:, lines(i), :].reshape(2 * chunk, cols), weight[0], weight[1])
            mixed[0, 0, lines(i), :] = re.astype(BF)
            mixed[0, 1, lines(i), :] = im.astype(BF)
            return 0

        lax.fori_loop(0, chunks, take, 0)

        def give(i, _):
            re, im = times(both[:, lines(i), :].reshape(2 * chunk, height), mixed[0, 0], mixed[0, 1])
            put(i, direct[0, lines(i), :] + re, direct[1, lines(i), :] + im)
            return 0

        lax.fori_loop(0, chunks, give, 0)

    tall = rows + 2 * PAD

    def own(q):
        return pl.ds(pl.multiple_of(q * rows, PAD), tall)

    def e_copy(d):
        q = (p + d) % n_c
        return remote(o_buf.at[h, :, own(q), :], ext.at[p], e_send.at[d], e_recv.at[p], at_cross(q))

    for d in range(1, n_c):
        e_copy(d).start()
    ext[p] = o_buf[h, :, own(p), :]
    for d in range(1, n_c):
        q = (p + d) % n_c
        remote(o_buf.at[h, :, own(q), :], ext.at[q], e_send.at[d], e_recv.at[q], at_cross(q)).wait_recv()

    column = lax.broadcasted_iota(jnp.int32, (rows, cols), 1)

    def sideways(v):
        before = jnp.where(column == 0, 0.0, pltpu.roll(v, 1, 1))
        after = jnp.where(column == cols - 1, 0.0, pltpu.roll(v, cols - 1, 1))
        return before + after

    for b in range(RHS):
        for c in range(2):
            f = jnp.concatenate([ext[b * group + j, c].astype(jnp.float32) for j in range(group)], axis=1)
            here = f[PAD : PAD + rows]
            updown = (pltpu.roll(f, 1, 0) + pltpu.roll(f, tall - 1, 0))[PAD : PAD + rows]
            faces = updown + sideways(here)
            corners = sideways(updown)
            sol_ref[c, 0, b] = here
            p_out[c, b] = (FACE * here + EDGE * faces + CORNER * corners).astype(BF)
            res_ref[c, 0, b] = rhs_ref[c, 0, b] - CENTER * here + (FACE * faces + EDGE * corners)

    def p_copy(way):
        to = jnp.maximum(sec - 1, 0) if way == 1 else jnp.minimum(sec + 1, n_s - 1)
        return remote(p_out, p_in.at[way], p_send.at[way], p_recv.at[way], at_sec(to))

    @pl.when(sec < n_s - 1)
    def _():
        p_copy(0).start()

    @pl.when(sec > 0)
    def _():
        p_copy(1).start()

    line = lax.broadcasted_iota(jnp.int32, (1, cols), 1)
    distance = jnp.minimum(line, cols - 1 - line).astype(jnp.float32)
    depth = jnp.full((1, cols), depth_ref[0], jnp.int32).astype(jnp.float32)
    ramp = jnp.maximum(depth - distance, 0.0) / depth
    damping = SIGMA_TOP * ramp * ramp
    wave_real = slow_ref[0]
    wave_imag = wave_real * damping
    for b in range(RHS):
        re, im = sol_ref[0, 0, b], sol_ref[1, 0, b]
        res_ref[0, 0, b] += wave_real * re - wave_imag * im
        res_ref[1, 0, b] += wave_real * im + wave_imag * re

    def neighbour(way):
        p_copy(way).wait_recv()
        for b in range(RHS):
            for c in range(2):
                res_ref[c, 0, b] += p_in[way, c, b].astype(jnp.float32)

    @pl.when(sec > 0)
    def _():
        neighbour(0)

    @pl.when(sec < n_s - 1)
    def _():
        neighbour(1)

    for t in range(n_c):
        is_a, a, is_z, z = places(t)
        for b in range(RHS):
            @pl.when(jnp.logical_and(is_a, moves_right(b)))
            def _():
                r_copy(b, a, 0, right).wait_send()

            @pl.when(jnp.logical_and(is_z, moves_left(b)))
            def _():
                r_copy(b, z, 1, left).wait_send()

        @pl.when(jnp.logical_and(is_a, p < last))
        def _():
            c_copy(a, 0, right).wait_send()

        @pl.when(jnp.logical_and(is_z, p > 0))
        def _():
            c_copy(z, 1, left).wait_send()

    def sent(i, _):
        @pl.when(hands_on)
        def _():
            s_copy(i).wait_send()

        @pl.when(jnp.logical_and(sec >= 2, odd == 1))
        def _():
            for d in range(1, group):
                y_copy(i, d).wait_send()
            for j in range(group):
                d_copy(i, j).wait_send()

        return 0

    @pl.when(odd == 0)
    def _():
        l_copy().wait_send()
        for q in range(n_c):
            f_copy(0, q).wait_send()
            f_copy(1, q).wait_send()

    lax.fori_loop(0, chunks, sent, 0)
    for d in range(1, n_c):
        e_copy(d).wait_send()

    @pl.when(sec < n_s - 1)
    def _():
        p_copy(0).wait_send()

    @pl.when(sec > 0)
    def _():
        p_copy(1).wait_send()


def per_device(n_s, n_c, rhs_field, slowness, absorb_depth, line_inverse, cross_inverse):
    rows, cols = slowness.shape[1:]
    height = rows * n_c
    group = n_c // RHS
    width = cols // group
    chunk = min(128, height)
    chunks = height // chunk
    vmem = pl.BlockSpec(memory_space=pltpu.VMEM)
    dma = pltpu.SemaphoreType.DMA
    out = jax.ShapeDtypeStruct(rhs_field.shape, jnp.float32)
    return pl.pallas_call(
        functools.partial(kernel, n_s, n_c),
        out_shape=(out, out),
        in_specs=[vmem, vmem, pl.BlockSpec(memory_space=pltpu.SMEM), vmem, vmem],
        out_specs=(vmem, vmem),
        scratch_shapes=[
            pltpu.VMEM((RHS, 2, height, cols), BF),
            pltpu.VMEM((2, height, height), BF),
            pltpu.VMEM((2, height, cols), BF),
            pltpu.VMEM((2, height, height), BF),
            pltpu.VMEM((2, cols, cols), BF),
            pltpu.VMEM((2, cols, width), BF),
            pltpu.VMEM((2, height, width), jnp.float32),
            pltpu.VMEM((2, height, cols), BF),
            pltpu.VMEM((2, height, height), BF),
            pltpu.VMEM((2, 2, height, width), BF),
            pltpu.VMEM((group, 2, height, width), BF),
            pltpu.VMEM((group, 2, height + 2 * PAD, width), BF),
            pltpu.VMEM((n_c, 2, rows + 2 * PAD, width), BF),
            pltpu.VMEM((2, RHS, rows, cols), BF),
            pltpu.VMEM((2, 2, RHS, rows, cols), BF),
            dma((2, n_c)), dma((n_c,)),
            dma((RHS, 2, n_c)), dma((RHS, n_c)),
            dma((2, n_c)), dma((2, n_c)), dma, dma,
            dma((chunks,)), dma((chunks, group)), dma((chunks, group)), dma((chunks, group)),
            dma((n_c,)), dma((n_c,)),
            dma((2,)), dma((2,)),
        ],
        compiler_params=pltpu.CompilerParams(
            collective_id=0, has_side_effects=True, vmem_limit_bytes=56 * 1024 * 1024
        ),
        name="sweep",
    )(rhs_field, slowness, absorb_depth, line_inverse, cross_inverse)


def solution(mesh):
    field = P(None, "sec", None, "cross", None)
    return jax.shard_map(
        functools.partial(per_device, mesh.shape["sec"], mesh.shape["cross"]),
        mesh=mesh,
        in_specs=(
            field,
            P("sec", "cross", None),
            P("sec"),
            P("sec", None, None, None),
            P("sec", None, "cross", None),
        ),
        out_specs=(field, field),
        check_vma=False,
    )
```

```python
import functools

import jax
import jax.numpy as jnp
from jax import lax
from jax.experimental import pallas as pl
from jax.experimental.pallas import tpu as pltpu
from jax.sharding import PartitionSpec as P

MESH = pl.DeviceIdType.MESH
SIGMA_TOP = 2.0
CENTER = 128.0 / 30.0
FACE = 14.0 / 30.0
EDGE = 3.0 / 30.0
CORNER = 1.0 / 30.0
PAD = 16
RHS = 2
BF = jnp.bfloat16


def kernel(
    n_s, n_c,
    rhs_ref, slow_ref, depth_ref, line_ref, cross_ref,
    sol_ref, res_ref,
    rhs_full, c_full, r_in, c_in, l_in, weight, direct, src, both, mixed, s_in, o_buf, ext, p_out, p_in,
    c_send, c_recv, r_send, r_recv, f_send, f_recv, l_send, l_recv,
    s_send, s_recv, y_send, d_send, e_send, e_recv, p_send, p_recv,
):
    rows, cols = slow_ref.shape[1], slow_ref.shape[2]
    height = rows * n_c
    group = n_c // RHS
    width = cols // group
    chunk = min(128, height)
    chunks = height // chunk
    sec = lax.axis_index("sec")
    p = lax.axis_index("cross")
    r = p // group
    h = p % group
    odd = sec % 2

    def remote(source, target, send, recv, where):
        return pltpu.make_async_remote_copy(
            src_ref=source, dst_ref=target, send_sem=send, recv_sem=recv,
            device_id=where, device_id_type=MESH,
        )

    def at_sec(s):
        return {"sec": s, "cross": p}

    def at_cross(q):
        return {"sec": sec, "cross": q}

    barrier = pltpu.get_barrier_semaphore()
    for d in range(1, n_c):
        pl.semaphore_signal(barrier, inc=1, device_id=at_cross((p + d) % n_c), device_id_type=MESH)

    @pl.when(sec > 0)
    def _():
        pl.semaphore_signal(barrier, inc=1, device_id=at_sec(sec - 1), device_id_type=MESH)

    @pl.when(sec < n_s - 1)
    def _():
        pl.semaphore_signal(barrier, inc=1, device_id=at_sec(sec + 1), device_id_type=MESH)

    @pl.when(jnp.logical_and(odd == 1, sec >= 2))
    def _():
        pl.semaphore_signal(barrier, inc=1, device_id=at_sec(sec - 2), device_id_type=MESH)

    @pl.when(jnp.logical_and(odd == 1, sec <= n_s - 3))
    def _():
        pl.semaphore_signal(barrier, inc=1, device_id=at_sec(sec + 2), device_id_type=MESH)

    def block(q):
        return pl.ds(pl.multiple_of(q * rows, rows), rows)

    for b in range(RHS):
        for c in range(2):
            rhs_full[b, c, block(p), :] = rhs_ref[c, 0, b].astype(BF)
    for c in range(2):
        c_full[c, block(p), :] = cross_ref[0, c]
    zeros_pad = jnp.zeros((PAD, width), BF)
    for j in range(group):
        for c in range(2):
            o_buf[j, c, 0:PAD, :] = zeros_pad
            o_buf[j, c, PAD + height : PAD + height + PAD, :] = zeros_pad

    nearest = jnp.minimum(sec, 1) + jnp.minimum(n_s - 1 - sec, 1)
    second = jnp.minimum(sec // 2, 1) + jnp.minimum((n_s - 1 - sec) // 2, 1)
    pl.semaphore_wait(barrier, n_c - 1 + nearest + odd * second)

    def c_copy(q, way, to):
        return remote(c_full.at[:, block(q), :], c_full.at[:, block(q), :], c_send.at[way, q], c_recv.at[q], at_cross(to))

    def r_copy(b, q, way, to):
        return remote(rhs_full.at[b, :, block(q), :], rhs_full.at[b, :, block(q), :], r_send.at[b, way, q], r_recv.at[b, q], at_cross(to))

    partner = sec + 1 - 2 * odd

    def f_copy(kind, q):
        source, target = (rhs_full.at[r], r_in) if kind == 0 else (c_full, c_in)
        return remote(
            source.at[:, block(q), :], target.at[:, block(q), :], f_send.at[kind, q], f_recv.at[kind, q], at_sec(partner)
        )

    def l_copy():
        return remote(line_ref.at[0], l_in, l_send, l_recv, at_sec(partner))

    def times(left, w0, w1):
        one = jnp.dot(left, w0, preferred_element_type=jnp.float32)
        two = jnp.dot(left, w1, preferred_element_type=jnp.float32)
        half = left.shape[0] // 2
        return one[:half] - two[half:], two[:half] + one[half:]

    def lines(i):
        return pl.ds(pl.multiple_of(i * chunk, chunk), chunk)

    def part(j):
        return pl.ds(pl.multiple_of(j * width, width), width)

    span = min(128, cols)

    def weights():
        @pl.when(odd == 0)
        def _():
            for c in range(2):
                weight[c] = line_ref[0, c, :, part(h)]

        @pl.when(odd == 1)
        def _():
            l_copy().wait_recv()

            def rows_of(i, _):
                at = pl.ds(pl.multiple_of(i * span, span), span)
                re, im = times(
                    l_in[:, at, :].reshape(2 * span, cols), line_ref[0, 0, :, part(h)], line_ref[0, 1, :, part(h)]
                )
                weight[0, at, :] = re.astype(BF)
                weight[1, at, :] = im.astype(BF)
                return 0

            lax.fori_loop(0, cols // span, rows_of, 0)

    @pl.when(odd == 0)
    def _():
        l_copy().start()

    def moves_right(b):
        return p < n_c - 1 if b == 1 else p + 1 < group

    def moves_left(b):
        return p > 0 if b == 0 else p - 1 >= group

    last = n_c - 1
    right = jnp.minimum(p + 1, last)
    left = jnp.maximum(p - 1, 0)

    def places(t):
        return p - t >= 0, jnp.maximum(p - t, 0), p + t <= last, jnp.minimum(p + t, last)

    def forward(kind, q, got):
        @pl.when(jnp.logical_and(got, odd == 0))
        def _():
            f_copy(kind, q).start()

    def relay_r(t):
        is_a, a, is_z, z = places(t)
        for b in (1, 0):
            if t > 0:
                got = is_a if b == 1 else jnp.logical_and(is_a, p < group)

                @pl.when(got)
                def _():
                    r_copy(b, a, 0, left).wait_recv()

                forward(0, a, jnp.logical_and(got, r == b))

            @pl.when(jnp.logical_and(is_a, moves_right(b)))
            def _():
                r_copy(b, a, 0, right).start()

        for b in (0, 1):
            if t > 0:
                got = is_z if b == 0 else jnp.logical_and(is_z, p >= group)

                @pl.when(got)
                def _():
                    r_copy(b, z, 1, right).wait_recv()

                forward(0, z, jnp.logical_and(got, r == b))

            @pl.when(jnp.logical_and(is_z, moves_left(b)))
            def _():
                r_copy(b, z, 1, left).start()

    def relay_c(t):
        is_a, a, is_z, z = places(t)
        if t > 0:
            @pl.when(is_a)
            def _():
                c_copy(a, 0, left).wait_recv()

            forward(1, a, is_a)

        @pl.when(jnp.logical_and(is_a, p < last))
        def _():
            c_copy(a, 0, right).start()

        if t > 0:
            @pl.when(is_z)
            def _():
                c_copy(z, 1, right).wait_recv()

            forward(1, z, is_z)

        @pl.when(jnp.logical_and(is_z, p > 0))
        def _():
            c_copy(z, 1, left).start()

    tall_chunk = min(256, height)

    def tall_lines(i):
        return pl.ds(pl.multiple_of(i * tall_chunk, tall_chunk), tall_chunk)

    def line_products():
        @pl.when(odd == 1)
        def _():
            for q in range(n_c):
                f_copy(0, q).wait_recv()

        def some(i, _):
            @pl.when(odd == 1)
            def _():
                re, im = times(
                    rhs_full[r, :, tall_lines(i), :].reshape(2 * tall_chunk, cols),
                    line_ref[0, 0, :, part(h)], line_ref[0, 1, :, part(h)],
                )
                direct[0, tall_lines(i), :] = re
                direct[1, tall_lines(i), :] = im
                src[:, tall_lines(i), :] = r_in[:, tall_lines(i), :]

            @pl.when(odd == 0)
            def _():
                src[:, tall_lines(i), :] = rhs_full[r, :, tall_lines(i), :]

            re, im = times(src[:, tall_lines(i), :].reshape(2 * tall_chunk, cols), weight[0], weight[1])
            mixed[odd, 0, tall_lines(i), :] = re.astype(BF)
            mixed[odd, 1, tall_lines(i), :] = im.astype(BF)
            return 0

        lax.fori_loop(0, height // tall_chunk, some, 0)

    relay_r(0)
    relay_c(0)
    forward(0, p, p >= 0)
    forward(1, p, p >= 0)
    weights()
    for t in range(1, n_c):
        relay_r(t)
    relay_c(1)
    line_products()
    for t in range(2, n_c):
        relay_c(t)

    def padded_lines(i):
        return pl.ds(pl.multiple_of(PAD + i * chunk, PAD), chunk)

    def s_copy(i):
        return remote(
            o_buf.at[h, :, padded_lines(i), :], s_in.at[h, :, lines(i), :], s_send.at[i], s_recv.at[i, h],
            at_sec(jnp.minimum(sec + 2, n_s - 1)),
        )

    def y_copy(i, d):
        other = r * group + (h + d) % group
        return remote(
            s_in.at[h, :, lines(i), :], s_in.at[h, :, lines(i), :], y_send.at[i, d], s_recv.at[i, h], at_cross(other)
        )

    def d_copy(i, j):
        return remote(
            s_in.at[j, :, lines(i), :], s_in.at[j, :, lines(i), :], d_send.at[i, j], s_recv.at[i, j], at_sec(partner)
        )

    @pl.when(odd == 1)
    def _():
        for q in range(n_c):
            f_copy(1, q).wait_recv()

        def even_layer(i, _):
            re, im = times(c_in[:, tall_lines(i), :].reshape(2 * tall_chunk, height), mixed[1, 0], mixed[1, 1])
            mixed[0, 0, tall_lines(i), :] = (direct[0, tall_lines(i), :] + re).astype(BF)
            mixed[0, 1, tall_lines(i), :] = (direct[1, tall_lines(i), :] + im).astype(BF)
            return 0

        lax.fori_loop(0, height // tall_chunk, even_layer, 0)

    tall = rows + 2 * PAD

    def own(q):
        return pl.ds(pl.multiple_of(q * rows, PAD), tall)

    def e_copy(to, whose):
        return remote(o_buf.at[h, :, own(to), :], ext.at[whose], e_send.at[to], e_recv.at[whose], at_cross(to))

    hands_on = jnp.logical_and(odd == 1, sec <= n_s - 3)

    def put(i, re, im):
        o_buf[h, 0, padded_lines(i), :] = re.astype(BF)
        o_buf[h, 1, padded_lines(i), :] = im.astype(BF)

        @pl.when(hands_on)
        def _():
            s_copy(i).start()

        for q in range(n_c):
            complete = min(((q + 1) * rows + PAD - 1) // chunk, chunks - 1)

            @pl.when(jnp.logical_and(i == complete, p != q))
            def _():
                e_copy(q, p).start()

    def alone(i, _):
        re, im = times(c_full[:, lines(i), :].reshape(2 * chunk, height), mixed[0, 0], mixed[0, 1])

        @pl.when(sec < 2)
        def _():
            put(i, re, im)

        @pl.when(sec >= 2)
        def _():
            direct[0, lines(i), :] = re
            direct[1, lines(i), :] = im

            @pl.when(odd == 0)
            def _():
                both[:, lines(i), :] = c_full[:, lines(i), :]

            @pl.when(odd == 1)
            def _():
                re, im = times(c_full[:, lines(i), :].reshape(2 * chunk, height), c_in[0], c_in[1])
                both[0, lines(i), :] = re.astype(BF)
                both[1, lines(i), :] = im.astype(BF)

        return 0

    lax.fori_loop(0, chunks, alone, 0)

    @pl.when(sec >= 2)
    def _():
        def pass_on(i, _):
            d_copy(i, h).wait_recv()

            @pl.when(odd == 1)
            def _():
                for d in range(1, group):
                    y_copy(i, d).start()
                d_copy(i, h).start()

            return 0

        lax.fori_loop(0, chunks, pass_on, 0)

        def take(i, _):
            for d in range(1, group):
                j = (h + d) % group
                d_copy(i, j).wait_recv()

                @pl.when(odd == 1)
                def _():
                    d_copy(i, j).start()

            for c in range(2):
                for j in range(group):
                    src[c, lines(i), j * width : (j + 1) * width] = s_in[j, c, lines(i), :]
            re, im = times(src[:, lines(i), :].reshape(2 * chunk, cols), weight[0], weight[1])
            mixed[0, 0, lines(i), :] = re.astype(BF)
            mixed[0, 1, lines(i), :] = im.astype(BF)
            return 0

        lax.fori_loop(0, chunks, take, 0)

        def give(i, _):
            re, im = times(both[:, lines(i), :].reshape(2 * chunk, height), mixed[0, 0], mixed[0, 1])
            put(i, direct[0, lines(i), :] + re, direct[1, lines(i), :] + im)
            return 0

        lax.fori_loop(0, chunks, give, 0)

    for q in range(n_c):
        @pl.when(p != q)
        def _():
            e_copy(q, q).wait_recv()

    ext[p] = o_buf[h, :, own(p), :]

    column = lax.broadcasted_iota(jnp.int32, (rows, cols), 1)

    def sideways(v):
        before = jnp.where(column == 0, 0.0, pltpu.roll(v, 1, 1))
        after = jnp.where(column == cols - 1, 0.0, pltpu.roll(v, cols - 1, 1))
        return before + after

    for b in range(RHS):
        for c in range(2):
            f = jnp.concatenate([ext[b * group + j, c].astype(jnp.float32) for j in range(group)], axis=1)
            here = f[PAD : PAD + rows]
            updown = (pltpu.roll(f, 1, 0) + pltpu.roll(f, tall - 1, 0))[PAD : PAD + rows]
            faces = updown + sideways(here)
            corners = sideways(updown)
            sol_ref[c, 0, b] = here
            p_out[c, b] = (FACE * here + EDGE * faces + CORNER * corners).astype(BF)
            res_ref[c, 0, b] = rhs_ref[c, 0, b] - CENTER * here + (FACE * faces + EDGE * corners)

    def p_copy(way):
        to = jnp.maximum(sec - 1, 0) if way == 1 else jnp.minimum(sec + 1, n_s - 1)
        return remote(p_out, p_in.at[way], p_send.at[way], p_recv.at[way], at_sec(to))

    @pl.when(sec < n_s - 1)
    def _():
        p_copy(0).start()

    @pl.when(sec > 0)
    def _():
        p_copy(1).start()

    line = lax.broadcasted_iota(jnp.int32, (1, cols), 1)
    distance = jnp.minimum(line, cols - 1 - line).astype(jnp.float32)
    depth = jnp.full((1, cols), depth_ref[0], jnp.int32).astype(jnp.float32)
    ramp = jnp.maximum(depth - distance, 0.0) / depth
    damping = SIGMA_TOP * ramp * ramp
    wave_real = slow_ref[0]
    wave_imag = wave_real * damping
    for b in range(RHS):
        re, im = sol_ref[0, 0, b], sol_ref[1, 0, b]
        res_ref[0, 0, b] += wave_real * re - wave_imag * im
        res_ref[1, 0, b] += wave_real * im + wave_imag * re

    def neighbour(way):
        p_copy(way).wait_recv()
        for b in range(RHS):
            for c in range(2):
                res_ref[c, 0, b] += p_in[way, c, b].astype(jnp.float32)

    @pl.when(sec > 0)
    def _():
        neighbour(0)

    @pl.when(sec < n_s - 1)
    def _():
        neighbour(1)

    for t in range(n_c):
        is_a, a, is_z, z = places(t)
        for b in range(RHS):
            @pl.when(jnp.logical_and(is_a, moves_right(b)))
            def _():
                r_copy(b, a, 0, right).wait_send()

            @pl.when(jnp.logical_and(is_z, moves_left(b)))
            def _():
                r_copy(b, z, 1, left).wait_send()

        @pl.when(jnp.logical_and(is_a, p < last))
        def _():
            c_copy(a, 0, right).wait_send()

        @pl.when(jnp.logical_and(is_z, p > 0))
        def _():
            c_copy(z, 1, left).wait_send()

    def sent(i, _):
        @pl.when(hands_on)
        def _():
            s_copy(i).wait_send()

        @pl.when(jnp.logical_and(sec >= 2, odd == 1))
        def _():
            for d in range(1, group):
                y_copy(i, d).wait_send()
            for j in range(group):
                d_copy(i, j).wait_send()

        return 0

    @pl.when(odd == 0)
    def _():
        l_copy().wait_send()
        for q in range(n_c):
            f_copy(0, q).wait_send()
            f_copy(1, q).wait_send()

    lax.fori_loop(0, chunks, sent, 0)
    for q in range(n_c):
        @pl.when(p != q)
        def _():
            e_copy(q, p).wait_send()


    @pl.when(sec < n_s - 1)
    def _():
        p_copy(0).wait_send()

    @pl.when(sec > 0)
    def _():
        p_copy(1).wait_send()


def per_device(n_s, n_c, rhs_field, slowness, absorb_depth, line_inverse, cross_inverse):
    rows, cols = slowness.shape[1:]
    height = rows * n_c
    group = n_c // RHS
    width = cols // group
    chunk = min(128, height)
    chunks = height // chunk
    vmem = pl.BlockSpec(memory_space=pltpu.VMEM)
    dma = pltpu.SemaphoreType.DMA
    out = jax.ShapeDtypeStruct(rhs_field.shape, jnp.float32)
    return pl.pallas_call(
        functools.partial(kernel, n_s, n_c),
        out_shape=(out, out),
        in_specs=[vmem, vmem, pl.BlockSpec(memory_space=pltpu.SMEM), vmem, vmem],
        out_specs=(vmem, vmem),
        scratch_shapes=[
            pltpu.VMEM((RHS, 2, height, cols), BF),
            pltpu.VMEM((2, height, height), BF),
            pltpu.VMEM((2, height, cols), BF),
            pltpu.VMEM((2, height, height), BF),
            pltpu.VMEM((2, cols, cols), BF),
            pltpu.VMEM((2, cols, width), BF),
            pltpu.VMEM((2, height, width), jnp.float32),
            pltpu.VMEM((2, height, cols), BF),
            pltpu.VMEM((2, height, height), BF),
            pltpu.VMEM((2, 2, height, width), BF),
            pltpu.VMEM((group, 2, height, width), BF),
            pltpu.VMEM((group, 2, height + 2 * PAD, width), BF),
            pltpu.VMEM((n_c, 2, rows + 2 * PAD, width), BF),
            pltpu.VMEM((2, RHS, rows, cols), BF),
            pltpu.VMEM((2, 2, RHS, rows, cols), BF),
            dma((2, n_c)), dma((n_c,)),
            dma((RHS, 2, n_c)), dma((RHS, n_c)),
            dma((2, n_c)), dma((2, n_c)), dma, dma,
            dma((chunks,)), dma((chunks, group)), dma((chunks, group)), dma((chunks, group)),
            dma((n_c,)), dma((n_c,)),
            dma((2,)), dma((2,)),
        ],
        compiler_params=pltpu.CompilerParams(
            collective_id=0, has_side_effects=True, vmem_limit_bytes=56 * 1024 * 1024
        ),
        name="sweep",
    )(rhs_field, slowness, absorb_depth, line_inverse, cross_inverse)


def solution(mesh):
    field = P(None, "sec", None, "cross", None)
    return jax.shard_map(
        functools.partial(per_device, mesh.shape["sec"], mesh.shape["cross"]),
        mesh=mesh,
        in_specs=(
            field,
            P("sec", "cross", None),
            P("sec"),
            P("sec", None, None, None),
            P("sec", None, "cross", None),
        ),
        out_specs=(field, field),
        check_vma=False,
    )
```

```python
import functools

import jax
import jax.numpy as jnp
from jax import lax
from jax.experimental import pallas as pl
from jax.experimental.pallas import tpu as pltpu
from jax.sharding import PartitionSpec as P

MESH = pl.DeviceIdType.MESH
SIGMA_TOP = 2.0
CENTER = 128.0 / 30.0
FACE = 14.0 / 30.0
EDGE = 3.0 / 30.0
CORNER = 1.0 / 30.0
PAD = 16
RHS = 2
BF = jnp.bfloat16


def kernel(
    n_s, n_c,
    rhs_ref, slow_ref, depth_ref, line_ref, cross_ref,
    sol_ref, res_ref,
    rhs_full, c_full, r_in, c_in, l_in, weight, direct, src, both, mixed, s_in, o_buf, ext, p_out, p_in,
    c_send, c_recv, r_send, r_recv, f_send, f_recv, l_send, l_recv,
    s_send, s_recv, y_send, d_send, e_send, e_recv, p_send, p_recv,
):
    rows, cols = slow_ref.shape[1], slow_ref.shape[2]
    height = rows * n_c
    group = n_c // RHS
    width = cols // group
    chunk = min(128, height)
    chunks = height // chunk
    sec = lax.axis_index("sec")
    p = lax.axis_index("cross")
    r = p // group
    h = p % group
    odd = sec % 2

    def remote(source, target, send, recv, where):
        return pltpu.make_async_remote_copy(
            src_ref=source, dst_ref=target, send_sem=send, recv_sem=recv,
            device_id=where, device_id_type=MESH,
        )

    def at_sec(s):
        return {"sec": s, "cross": p}

    def at_cross(q):
        return {"sec": sec, "cross": q}

    barrier = pltpu.get_barrier_semaphore()
    for d in range(1, n_c):
        pl.semaphore_signal(barrier, inc=1, device_id=at_cross((p + d) % n_c), device_id_type=MESH)

    @pl.when(sec > 0)
    def _():
        pl.semaphore_signal(barrier, inc=1, device_id=at_sec(sec - 1), device_id_type=MESH)

    @pl.when(sec < n_s - 1)
    def _():
        pl.semaphore_signal(barrier, inc=1, device_id=at_sec(sec + 1), device_id_type=MESH)

    @pl.when(jnp.logical_and(odd == 1, sec >= 2))
    def _():
        pl.semaphore_signal(barrier, inc=1, device_id=at_sec(sec - 2), device_id_type=MESH)

    @pl.when(jnp.logical_and(odd == 1, sec <= n_s - 3))
    def _():
        pl.semaphore_signal(barrier, inc=1, device_id=at_sec(sec + 2), device_id_type=MESH)

    def block(q):
        return pl.ds(pl.multiple_of(q * rows, rows), rows)

    for b in range(RHS):
        for c in range(2):
            rhs_full[b, c, block(p), :] = rhs_ref[c, 0, b].astype(BF)
    for c in range(2):
        c_full[c, block(p), :] = cross_ref[0, c]
    zeros_pad = jnp.zeros((PAD, width), BF)
    for j in range(group):
        for c in range(2):
            o_buf[j, c, 0:PAD, :] = zeros_pad
            o_buf[j, c, PAD + height : PAD + height + PAD, :] = zeros_pad

    nearest = jnp.minimum(sec, 1) + jnp.minimum(n_s - 1 - sec, 1)
    second = jnp.minimum(sec // 2, 1) + jnp.minimum((n_s - 1 - sec) // 2, 1)
    pl.semaphore_wait(barrier, n_c - 1 + nearest + odd * second)

    def c_copy(q, way, to):
        return remote(c_full.at[:, block(q), :], c_full.at[:, block(q), :], c_send.at[way, q], c_recv.at[q], at_cross(to))

    def r_copy(b, q, way, to):
        return remote(rhs_full.at[b, :, block(q), :], rhs_full.at[b, :, block(q), :], r_send.at[b, way, q], r_recv.at[b, q], at_cross(to))

    partner = sec + 1 - 2 * odd

    def f_copy(kind, q):
        source, target = (rhs_full.at[r], r_in) if kind == 0 else (c_full, c_in)
        return remote(
            source.at[:, block(q), :], target.at[:, block(q), :], f_send.at[kind, q], f_recv.at[kind, q], at_sec(partner)
        )

    def l_copy():
        return remote(line_ref.at[0], l_in, l_send, l_recv, at_sec(partner))

    def times(left, w0, w1):
        one = jnp.dot(left, w0, preferred_element_type=jnp.float32)
        two = jnp.dot(left, w1, preferred_element_type=jnp.float32)
        half = left.shape[0] // 2
        return one[:half] - two[half:], two[:half] + one[half:]

    def lines(i):
        return pl.ds(pl.multiple_of(i * chunk, chunk), chunk)

    def part(j):
        return pl.ds(pl.multiple_of(j * width, width), width)

    span = min(128, cols)

    def weights():
        @pl.when(odd == 0)
        def _():
            for c in range(2):
                weight[c] = line_ref[0, c, :, part(h)]

        @pl.when(odd == 1)
        def _():
            l_copy().wait_recv()

            def rows_of(i, _):
                at = pl.ds(pl.multiple_of(i * span, span), span)
                re, im = times(
                    l_in[:, at, :].reshape(2 * span, cols), line_ref[0, 0, :, part(h)], line_ref[0, 1, :, part(h)]
                )
                weight[0, at, :] = re.astype(BF)
                weight[1, at, :] = im.astype(BF)
                return 0

            lax.fori_loop(0, cols // span, rows_of, 0)

    @pl.when(odd == 0)
    def _():
        l_copy().start()

    def moves_right(b):
        return p < n_c - 1 if b == 1 else p + 1 < group

    def moves_left(b):
        return p > 0 if b == 0 else p - 1 >= group

    last = n_c - 1
    right = jnp.minimum(p + 1, last)
    left = jnp.maximum(p - 1, 0)

    def places(t):
        return p - t >= 0, jnp.maximum(p - t, 0), p + t <= last, jnp.minimum(p + t, last)

    def forward(kind, q, got):
        @pl.when(jnp.logical_and(got, odd == 0))
        def _():
            f_copy(kind, q).start()

    def relay_r(t):
        is_a, a, is_z, z = places(t)
        for b in (1, 0):
            if t > 0:
                got = is_a if b == 1 else jnp.logical_and(is_a, p < group)

                @pl.when(got)
                def _():
                    r_copy(b, a, 0, left).wait_recv()

                forward(0, a, jnp.logical_and(got, r == b))

            @pl.when(jnp.logical_and(is_a, moves_right(b)))
            def _():
                r_copy(b, a, 0, right).start()

        for b in (0, 1):
            if t > 0:
                got = is_z if b == 0 else jnp.logical_and(is_z, p >= group)

                @pl.when(got)
                def _():
                    r_copy(b, z, 1, right).wait_recv()

                forward(0, z, jnp.logical_and(got, r == b))

            @pl.when(jnp.logical_and(is_z, moves_left(b)))
            def _():
                r_copy(b, z, 1, left).start()

    def relay_c(t):
        is_a, a, is_z, z = places(t)
        if t > 0:
            @pl.when(is_a)
            def _():
                c_copy(a, 0, left).wait_recv()

            forward(1, a, is_a)

        @pl.when(jnp.logical_and(is_a, p < last))
        def _():
            c_copy(a, 0, right).start()

        if t > 0:
            @pl.when(is_z)
            def _():
                c_copy(z, 1, right).wait_recv()

            forward(1, z, is_z)

        @pl.when(jnp.logical_and(is_z, p > 0))
        def _():
            c_copy(z, 1, left).start()

    tall_chunk = min(256, height)

    def tall_lines(i):
        return pl.ds(pl.multiple_of(i * tall_chunk, tall_chunk), tall_chunk)

    def line_products():
        @pl.when(odd == 1)
        def _():
            for q in range(n_c):
                f_copy(0, q).wait_recv()

        def some(i, _):
            @pl.when(odd == 1)
            def _():
                re, im = times(
                    rhs_full[r, :, tall_lines(i), :].reshape(2 * tall_chunk, cols),
                    line_ref[0, 0, :, part(h)], line_ref[0, 1, :, part(h)],
                )
                direct[0, tall_lines(i), :] = re
                direct[1, tall_lines(i), :] = im
                src[:, tall_lines(i), :] = r_in[:, tall_lines(i), :]

            @pl.when(odd == 0)
            def _():
                src[:, tall_lines(i), :] = rhs_full[r, :, tall_lines(i), :]

            re, im = times(src[:, tall_lines(i), :].reshape(2 * tall_chunk, cols), weight[0], weight[1])
            mixed[odd, 0, tall_lines(i), :] = re.astype(BF)
            mixed[odd, 1, tall_lines(i), :] = im.astype(BF)
            return 0

        lax.fori_loop(0, height // tall_chunk, some, 0)

    relay_r(0)
    relay_c(0)
    forward(0, p, p >= 0)
    forward(1, p, p >= 0)
    weights()
    for t in range(1, n_c):
        relay_r(t)
    relay_c(1)
    line_products()
    for t in range(2, n_c):
        relay_c(t)

    def padded_lines(i):
        return pl.ds(pl.multiple_of(PAD + i * chunk, PAD), chunk)

    def s_copy(i):
        return remote(
            o_buf.at[h, :, padded_lines(i), :], s_in.at[h, :, lines(i), :], s_send.at[i], s_recv.at[i, h],
            at_sec(jnp.minimum(sec + 2, n_s - 1)),
        )

    def y_copy(i, d):
        other = r * group + (h + d) % group
        return remote(
            s_in.at[h, :, lines(i), :], s_in.at[h, :, lines(i), :], y_send.at[i, d], s_recv.at[i, h], at_cross(other)
        )

    def d_copy(i, j):
        return remote(
            s_in.at[j, :, lines(i), :], s_in.at[j, :, lines(i), :], d_send.at[i, j], s_recv.at[i, j], at_sec(partner)
        )

    @pl.when(odd == 1)
    def _():
        for q in range(n_c):
            f_copy(1, q).wait_recv()

        def even_layer(i, _):
            re, im = times(c_in[:, tall_lines(i), :].reshape(2 * tall_chunk, height), mixed[1, 0], mixed[1, 1])
            mixed[0, 0, tall_lines(i), :] = (direct[0, tall_lines(i), :] + re).astype(BF)
            mixed[0, 1, tall_lines(i), :] = (direct[1, tall_lines(i), :] + im).astype(BF)
            return 0

        lax.fori_loop(0, height // tall_chunk, even_layer, 0)

    tall = rows + 2 * PAD

    def own(q):
        return pl.ds(pl.multiple_of(q * rows, PAD), tall)

    def e_copy(to, whose):
        return remote(o_buf.at[h, :, own(to), :], ext.at[whose], e_send.at[to], e_recv.at[whose], at_cross(to))

    hands_on = jnp.logical_and(odd == 1, sec <= n_s - 3)

    def put(i, re, im):
        o_buf[h, 0, padded_lines(i), :] = re.astype(BF)
        o_buf[h, 1, padded_lines(i), :] = im.astype(BF)

        @pl.when(hands_on)
        def _():
            s_copy(i).start()

        for q in range(n_c):
            complete = min(((q + 1) * rows + PAD - 1) // chunk, chunks - 1)

            @pl.when(jnp.logical_and(i == complete, p != q))
            def _():
                e_copy(q, p).start()

    def alone(i, _):
        re, im = times(c_full[:, lines(i), :].reshape(2 * chunk, height), mixed[0, 0], mixed[0, 1])

        @pl.when(sec < 2)
        def _():
            put(i, re, im)

        @pl.when(sec >= 2)
        def _():
            direct[0, lines(i), :] = re
            direct[1, lines(i), :] = im

        return 0

    lax.fori_loop(0, chunks, alone, 0)

    @pl.when(sec >= 2)
    def _():
        def pass_on(i, _):
            d_copy(i, h).wait_recv()

            @pl.when(odd == 1)
            def _():
                for d in range(1, group):
                    y_copy(i, d).start()
                d_copy(i, h).start()

            return 0

        def compose(i, _):
            @pl.when(odd == 0)
            def _():
                both[:, lines(i), :] = c_full[:, lines(i), :]

            @pl.when(odd == 1)
            def _():
                re, im = times(c_full[:, lines(i), :].reshape(2 * chunk, height), c_in[0], c_in[1])
                both[0, lines(i), :] = re.astype(BF)
                both[1, lines(i), :] = im.astype(BF)

            return 0

        @pl.when(sec < 4)
        def _():
            lax.fori_loop(0, chunks, pass_on, 0)

        lax.fori_loop(0, chunks, compose, 0)

        @pl.when(sec >= 4)
        def _():
            lax.fori_loop(0, chunks, pass_on, 0)

        def take(i, _):
            for d in range(1, group):
                j = (h + d) % group
                d_copy(i, j).wait_recv()

                @pl.when(odd == 1)
                def _():
                    d_copy(i, j).start()

            for c in range(2):
                for j in range(group):
                    src[c, lines(i), j * width : (j + 1) * width] = s_in[j, c, lines(i), :]
            re, im = times(src[:, lines(i), :].reshape(2 * chunk, cols), weight[0], weight[1])
            mixed[0, 0, lines(i), :] = re.astype(BF)
            mixed[0, 1, lines(i), :] = im.astype(BF)
            return 0

        lax.fori_loop(0, chunks, take, 0)

        def give(i, _):
            re, im = times(both[:, lines(i), :].reshape(2 * chunk, height), mixed[0, 0], mixed[0, 1])
            put(i, direct[0, lines(i), :] + re, direct[1, lines(i), :] + im)
            return 0

        lax.fori_loop(0, chunks, give, 0)

    for q in range(n_c):
        @pl.when(p != q)
        def _():
            e_copy(q, q).wait_recv()

    ext[p] = o_buf[h, :, own(p), :]

    column = lax.broadcasted_iota(jnp.int32, (rows, cols), 1)

    def sideways(v):
        before = jnp.where(column == 0, 0.0, pltpu.roll(v, 1, 1))
        after = jnp.where(column == cols - 1, 0.0, pltpu.roll(v, cols - 1, 1))
        return before + after

    for b in range(RHS):
        for c in range(2):
            f = jnp.concatenate([ext[b * group + j, c].astype(jnp.float32) for j in range(group)], axis=1)
            here = f[PAD : PAD + rows]
            updown = (pltpu.roll(f, 1, 0) + pltpu.roll(f, tall - 1, 0))[PAD : PAD + rows]
            faces = updown + sideways(here)
            corners = sideways(updown)
            sol_ref[c, 0, b] = here
            p_out[c, b] = (FACE * here + EDGE * faces + CORNER * corners).astype(BF)
            res_ref[c, 0, b] = rhs_ref[c, 0, b] - CENTER * here + (FACE * faces + EDGE * corners)

    def p_copy(way):
        to = jnp.maximum(sec - 1, 0) if way == 1 else jnp.minimum(sec + 1, n_s - 1)
        return remote(p_out, p_in.at[way], p_send.at[way], p_recv.at[way], at_sec(to))

    @pl.when(sec < n_s - 1)
    def _():
        p_copy(0).start()

    @pl.when(sec > 0)
    def _():
        p_copy(1).start()

    line = lax.broadcasted_iota(jnp.int32, (1, cols), 1)
    distance = jnp.minimum(line, cols - 1 - line).astype(jnp.float32)
    depth = jnp.full((1, cols), depth_ref[0], jnp.int32).astype(jnp.float32)
    ramp = jnp.maximum(depth - distance, 0.0) / depth
    damping = SIGMA_TOP * ramp * ramp
    wave_real = slow_ref[0]
    wave_imag = wave_real * damping
    for b in range(RHS):
        re, im = sol_ref[0, 0, b], sol_ref[1, 0, b]
        res_ref[0, 0, b] += wave_real * re - wave_imag * im
        res_ref[1, 0, b] += wave_real * im + wave_imag * re

    def neighbour(way):
        p_copy(way).wait_recv()
        for b in range(RHS):
            for c in range(2):
                res_ref[c, 0, b] += p_in[way, c, b].astype(jnp.float32)

    @pl.when(sec > 0)
    def _():
        neighbour(0)

    @pl.when(sec < n_s - 1)
    def _():
        neighbour(1)

    for t in range(n_c):
        is_a, a, is_z, z = places(t)
        for b in range(RHS):
            @pl.when(jnp.logical_and(is_a, moves_right(b)))
            def _():
                r_copy(b, a, 0, right).wait_send()

            @pl.when(jnp.logical_and(is_z, moves_left(b)))
            def _():
                r_copy(b, z, 1, left).wait_send()

        @pl.when(jnp.logical_and(is_a, p < last))
        def _():
            c_copy(a, 0, right).wait_send()

        @pl.when(jnp.logical_and(is_z, p > 0))
        def _():
            c_copy(z, 1, left).wait_send()

    def sent(i, _):
        @pl.when(hands_on)
        def _():
            s_copy(i).wait_send()

        @pl.when(jnp.logical_and(sec >= 2, odd == 1))
        def _():
            for d in range(1, group):
                y_copy(i, d).wait_send()
            for j in range(group):
                d_copy(i, j).wait_send()

        return 0

    @pl.when(odd == 0)
    def _():
        l_copy().wait_send()
        for q in range(n_c):
            f_copy(0, q).wait_send()
            f_copy(1, q).wait_send()

    lax.fori_loop(0, chunks, sent, 0)
    for q in range(n_c):
        @pl.when(p != q)
        def _():
            e_copy(q, p).wait_send()


    @pl.when(sec < n_s - 1)
    def _():
        p_copy(0).wait_send()

    @pl.when(sec > 0)
    def _():
        p_copy(1).wait_send()


def per_device(n_s, n_c, rhs_field, slowness, absorb_depth, line_inverse, cross_inverse):
    rows, cols = slowness.shape[1:]
    height = rows * n_c
    group = n_c // RHS
    width = cols // group
    chunk = min(128, height)
    chunks = height // chunk
    vmem = pl.BlockSpec(memory_space=pltpu.VMEM)
    dma = pltpu.SemaphoreType.DMA
    out = jax.ShapeDtypeStruct(rhs_field.shape, jnp.float32)
    return pl.pallas_call(
        functools.partial(kernel, n_s, n_c),
        out_shape=(out, out),
        in_specs=[vmem, vmem, pl.BlockSpec(memory_space=pltpu.SMEM), vmem, vmem],
        out_specs=(vmem, vmem),
        scratch_shapes=[
            pltpu.VMEM((RHS, 2, height, cols), BF),
            pltpu.VMEM((2, height, height), BF),
            pltpu.VMEM((2, height, cols), BF),
            pltpu.VMEM((2, height, height), BF),
            pltpu.VMEM((2, cols, cols), BF),
            pltpu.VMEM((2, cols, width), BF),
            pltpu.VMEM((2, height, width), jnp.float32),
            pltpu.VMEM((2, height, cols), BF),
            pltpu.VMEM((2, height, height), BF),
            pltpu.VMEM((2, 2, height, width), BF),
            pltpu.VMEM((group, 2, height, width), BF),
            pltpu.VMEM((group, 2, height + 2 * PAD, width), BF),
            pltpu.VMEM((n_c, 2, rows + 2 * PAD, width), BF),
            pltpu.VMEM((2, RHS, rows, cols), BF),
            pltpu.VMEM((2, 2, RHS, rows, cols), BF),
            dma((2, n_c)), dma((n_c,)),
            dma((RHS, 2, n_c)), dma((RHS, n_c)),
            dma((2, n_c)), dma((2, n_c)), dma, dma,
            dma((chunks,)), dma((chunks, group)), dma((chunks, group)), dma((chunks, group)),
            dma((n_c,)), dma((n_c,)),
            dma((2,)), dma((2,)),
        ],
        compiler_params=pltpu.CompilerParams(
            collective_id=0, has_side_effects=True, vmem_limit_bytes=56 * 1024 * 1024
        ),
        name="sweep",
    )(rhs_field, slowness, absorb_depth, line_inverse, cross_inverse)


def solution(mesh):
    field = P(None, "sec", None, "cross", None)
    return jax.shard_map(
        functools.partial(per_device, mesh.shape["sec"], mesh.shape["cross"]),
        mesh=mesh,
        in_specs=(
            field,
            P("sec", "cross", None),
            P("sec"),
            P("sec", None, None, None),
            P("sec", None, "cross", None),
        ),
        out_specs=(field, field),
        check_vma=False,
    )
```
